512 devices in a mesh: leaf: 128 (over z, y, core), near: 4 (over x).
Axes of the slice: x: 4, y: 8, z: 8, core: 2. Of those that a mesh axis runs over, the one named last changes fastest.
Arguments:
- bases: float32 [1024, 64, 64], P('leaf'), may hold values from -1 to 4
- leaf_transfer: float32 [1024, 64, 64], P('leaf'), may hold values from -1 to 4
- top_transfer: float32 [512, 64, 64], P('leaf'), may hold values from -1 to 4
- couplings: bfloat16 [65536, 64, 64], P(('leaf', 'near')), may hold values from -6 to 6
- coupling_target: int32 [65536], P(('leaf', 'near')), may hold values from 0 to 7
- coupling_dest: int32 [65536, 1], P(('leaf', 'near')), may hold values from 0 to 127; in each aligned block of 128 rows (0 to 127, 128 to 255, ...) at most 2 rows name the same one
- coupling_local: int32 [65536], P(('leaf', 'near')), may hold values from 0 to 7
- top_couplings: bfloat16 [8192, 64, 64], P(('leaf', 'near')), may hold values from -0.59765625 to 0.59765625
- top_target: int32 [8192], P(('leaf', 'near')), may hold values from 0 to 7
- top_source: int32 [8192], P(('leaf', 'near')), may hold values from 0 to 255
Outputs:
- leaf_bases: float32 [1024, 64, 64], P(('leaf', 'near'))
- leaf_transfers: float32 [1024, 64, 64], P('leaf')
- top_transfers: float32 [512, 64, 64], P('leaf')
- new_couplings: bfloat16 [65536, 64, 64], P(('leaf', 'near'))
- new_top_couplings: bfloat16 [8192, 64, 64], P(('leaf', 'near'))
The draws below stay inside these ranges and needn't reach their ends.
Inputs may be any that keep to these rules, and one draw needn't show every extreme that they name: `coupling_dest`: among the leaf blocks of one device, at most 2 have their source in the same subtree.
All inputs are finite; a program needn't handle non-finite values.
Results may differ from the reference program's by a relative error of at most 0.0065.
Values may be sent and summed in bfloat16 or wider, within the bound.
A program may use at most 128 MiB of HBM per device.

```python
import math
import jax
import jax.numpy as jnp
import numpy as np
from jax import lax

RANK = 64
LEAF_PTS = 64
LEAF_DEV = 8
BLK_DEV = 128
TOP_DEV = 16
CAP = 2
LEAVES = 1024
MIDS = 512
TOPS = 256
ROWS = 65536
TOP_ROWS = 8192
N_LEAF = 128
N_NEAR = 4


def dominant(key, batch_count, row_count, col_count):
    key_diagonal, key_rest = jax.random.split(key)
    spread_scale = 0.6 / math.sqrt(col_count)
    diagonal = jax.random.uniform(key_diagonal, (batch_count, 1, col_count), jnp.float32, 1.0, 2.0)
    off_diagonal = jnp.clip(jax.random.normal(key_rest, (batch_count, row_count, col_count), jnp.float32), -4.0, 4.0)
    identity = jnp.eye(row_count, col_count, dtype=jnp.float32)
    return identity * diagonal + spread_scale * off_diagonal


def draw_bases(key, part):
    return dominant(jax.random.fold_in(key, 11), LEAVES, LEAF_PTS, RANK)


def draw_leaf_transfer(key, part):
    return dominant(jax.random.fold_in(key, 23), LEAVES, RANK, RANK)


def draw_top_transfer(key, part):
    return dominant(jax.random.fold_in(key, 37), MIDS, RANK, RANK)


def touch_ends(array, stream_key, least, high):
    shape = array.shape
    spot = [jax.random.randint(jax.random.fold_in(stream_key, axis), (), 0, shape[axis]) for axis in range(len(shape))]
    array = array.at[tuple(spot)].set(least)
    longest = shape.index(max(shape))
    spot[longest] = (spot[longest] + 1) % shape[longest]
    return array.at[tuple(spot)].set(high)


def levels(rng, shape, cuts, smallest, largest):
    def one(dim, shards_of):
        draws = jax.random.uniform(jax.random.fold_in(jax.random.fold_in(rng, 6), dim), (shards_of,), jnp.float32, smallest / len(cuts), largest / len(cuts))
        return jnp.repeat(jnp.exp(draws), shape[dim] // shards_of).reshape((-1,) + (1,) * (len(shape) - dim - 1))

    gain = one(*cuts[0])
    for cut in cuts[1:]:
        gain = gain * one(*cut)
    return gain


def assign_block(own_key, own, number, rows, amount, top, limit, slope):
    order = jax.random.permutation(own_key, amount)
    crowded, common = load_shares(amount, rows * top, limit, slope, True), load_shares(amount, rows * top, limit, slope, False)
    places = jnp.arange(amount)

    def named(lengths, offset_by):
        used = int((lengths > 0).sum())
        fixed = max(1, used // 4)
        moved = fixed + (places - fixed + offset_by * (used - fixed)) % max(1, amount - fixed)
        return jnp.zeros((amount,), jnp.int32).at[order[jnp.where(places < fixed, places, moved)]].set(jnp.asarray(lengths, jnp.int32))

    lengths = jnp.where(number % 4 == 0, named(crowded, number // 4), named(common, number - number // 4 - 1))
    mixed = jax.random.permutation(jax.random.fold_in(own, 3), amount)
    giver, receiver = mixed[0:amount // 2 * 2:2], mixed[1:amount // 2 * 2:2]
    slack = jnp.minimum(lengths[giver] - 1, limit - lengths[receiver]) // 2
    slack = jnp.where((giver == order[0]) | (receiver == order[0]) | (lengths[receiver] == 0), 0, jnp.maximum(slack, 0))
    moved = jax.random.randint(jax.random.fold_in(own, 4), (amount // 2,), 0, 1 << 20) % (slack + 1)
    lengths = lengths.at[giver].add(-moved).at[receiver].add(moved)
    items = jnp.searchsorted(jnp.cumsum(lengths), jnp.arange(rows * top), side="right").astype(jnp.int32)
    grid = items.reshape(top, rows).T
    grid = grid[jax.random.permutation(jax.random.fold_in(own, 1), rows)]
    offset_by = jax.random.randint(jax.random.fold_in(own, 2), (rows, 1), 0, top)
    return jnp.take_along_axis(grid, (jnp.arange(top)[None, :] + offset_by) % top, axis=1)


def load_shares(amount, total, most, slope, full):
    portions = [(1 << 20) // math.isqrt(grade ** slope) + 1 for grade in range(1, amount + 1)]
    largest = most if full else min(most, max(-(-total // amount), total * portions[0] // sum(portions)))
    least = 1 if total - largest >= amount - 1 else 0
    holding, surplus = [largest] + [least] * (amount - 1), total - largest - least * (amount - 1)
    while surplus > 0:
        movable = [i for i in range(1, amount) if holding[i] < largest] or [i for i in range(1, amount) if holding[i] < most]
        mass, left = sum([portions[i] for i in movable]), surplus
        for i in movable:
            more = min(most - holding[i], max(1, left * portions[i] // mass), surplus)
            holding[i] = holding[i] + more
            surplus = surplus - more
    return np.array(holding)


def bell_draw(own_key, dims, scale, bound, cuts=(), kind=jnp.bfloat16):
    array = jax.random.normal(own_key, dims, jnp.float32) * scale
    if len(cuts) > 0:
        array = levels(own_key, dims, cuts, -0.22, 0.18) * array
    return jnp.clip(array, min=-bound, max=bound).astype(kind)


def setup_inputs(seed: int = 0) -> dict:
    seeds = jax.random.split(jax.random.key(seed), 11)
    bases = draw_bases(jax.random.fold_in(seeds[10], 71), 0)
    leaf_transfer = draw_leaf_transfer(jax.random.fold_in(seeds[10], 71), 0)
    top_transfer = draw_top_transfer(jax.random.fold_in(seeds[10], 71), 0)
    couplings = bell_draw(seeds[3], (ROWS, RANK, RANK), 1.0, 6.0, ((0, 512),))
    coupling_target = touch_ends(jax.random.randint(seeds[4], (ROWS,), 0, LEAF_DEV), jax.random.fold_in(seeds[4], 1), 0, LEAF_DEV - 1).astype(jnp.int32)
    coupling_dest_keys = jax.random.split(jax.random.fold_in(seeds[5], 1), ROWS // BLK_DEV)
    coupling_dest_turns = jax.random.permutation(jax.random.fold_in(seeds[5], 3), ROWS // BLK_DEV)
    coupling_dest = jax.vmap(lambda own, number: assign_block(jax.random.fold_in(seeds[5], 2), own, number, BLK_DEV, N_LEAF, 1, CAP, 2))(coupling_dest_keys, coupling_dest_turns).reshape((ROWS, 1))
    coupling_local = touch_ends(jax.random.randint(seeds[6], (ROWS,), 0, LEAF_DEV), jax.random.fold_in(seeds[6], 1), 0, LEAF_DEV - 1).astype(jnp.int32)
    top_couplings = bell_draw(seeds[7], (TOP_ROWS, RANK, RANK), 0.1, 0.59765625, ((0, 512),))
    top_target = touch_ends(jax.random.randint(seeds[8], (TOP_ROWS,), 0, LEAF_DEV), jax.random.fold_in(seeds[8], 1), 0, LEAF_DEV - 1).astype(jnp.int32)
    top_source = touch_ends(jax.random.randint(seeds[9], (TOP_ROWS,), 0, TOPS), jax.random.fold_in(seeds[9], 1), 0, TOPS - 1).astype(jnp.int32)
    return dict(bases=bases, leaf_transfer=leaf_transfer, top_transfer=top_transfer, couplings=couplings, coupling_target=coupling_target, coupling_dest=coupling_dest, coupling_local=coupling_local, top_couplings=top_couplings, top_target=top_target, top_source=top_source)


exact_mode = lax.Precision.HIGHEST

def gram_of(stacked):
    return jnp.einsum('nmk,nml->nkl', stacked, stacked, precision=exact_mode)

def right_solve(lower_part, stacked):

    def single(factor_one, block_one):
        return jax.scipy.linalg.solve_triangular(factor_one, block_one.T, lower=True).T
    return jax.vmap(single)(lower_part, stacked)

def merge_level(pieces, groups, width):
    paired = pieces.reshape(groups, 2, width, RANK, RANK)
    first_child = paired[:, 0].reshape(groups * width, RANK, RANK)
    second_child = paired[:, 1].reshape(groups * width, RANK, RANK)
    lower_part = jnp.linalg.cholesky(gram_of(first_child) + gram_of(second_child))
    spread = jnp.broadcast_to(lower_part.reshape(groups, 1, width, RANK, RANK), paired.shape)
    transfers = right_solve(spread.reshape(-1, RANK, RANK), pieces)
    return (transfers, jnp.swapaxes(lower_part, 1, 2))

def project(table, target_ids, source_ids, blocks, per_group):
    count = blocks.shape[0] // per_group

    def one_group(inputs):
        targets, sources, block_set = inputs
        left_rows = table[targets].astype(jnp.float32)
        right_rows = table[sources].astype(jnp.float32)
        halves = jnp.einsum('nkr,nrl->nkl', left_rows, block_set.astype(jnp.float32)).astype(jnp.bfloat16)
        return jnp.einsum('nkr,nlr->nkl', halves.astype(jnp.float32), right_rows).astype(jnp.bfloat16)
    result = lax.map(one_group, (target_ids.reshape(count, per_group), source_ids.reshape(count, per_group), blocks.reshape(count, per_group, RANK, RANK)))
    return result.reshape(blocks.shape)

def reference(bases, leaf_transfer, top_transfer, couplings, coupling_target, coupling_dest, coupling_local, top_couplings, top_target, top_source):
    lower_leaf = jnp.linalg.cholesky(gram_of(bases))
    leaf_bases = right_solve(lower_leaf, bases)
    leaf_factor = jnp.swapaxes(lower_leaf, 1, 2)
    child_piece = jnp.einsum('nkr,nrl->nkl', leaf_factor, leaf_transfer, precision=exact_mode)
    leaf_transfers, mid_factor = merge_level(child_piece, N_LEAF // 2, LEAF_DEV)
    up_piece = jnp.einsum('nkr,nrl->nkl', mid_factor, top_transfer, precision=exact_mode)
    top_transfers, top_factor = merge_level(up_piece, N_LEAF // 4, LEAF_DEV)
    leaf_low = leaf_factor.astype(jnp.bfloat16)
    top_low = top_factor.astype(jnp.bfloat16)
    row_index = jnp.arange(couplings.shape[0], dtype=jnp.int32)
    subtree = row_index // (N_NEAR * BLK_DEV)
    leaf_targets = subtree * LEAF_DEV + coupling_target
    leaf_sources = coupling_dest[:, 0] * LEAF_DEV + coupling_local
    new_couplings = project(leaf_low, leaf_targets, leaf_sources, couplings, BLK_DEV)
    top_index = jnp.arange(top_couplings.shape[0], dtype=jnp.int32)
    top_subtree = top_index // (N_NEAR * TOP_DEV)
    top_targets = top_subtree // 4 * LEAF_DEV + top_target
    new_top_couplings = project(top_low, top_targets, top_source, top_couplings, TOP_DEV)
    return (leaf_bases, leaf_transfers, top_transfers, new_couplings, new_top_couplings)
```

```python
import functools

import jax
import jax.numpy as jnp
from jax import lax
from jax.experimental import pallas as pl
from jax.experimental.pallas import tpu as pltpu
from jax.sharding import PartitionSpec as P

MESH = pl.DeviceIdType.MESH
F32 = jnp.float32
BF16 = jnp.bfloat16
EXACT = lax.Precision.HIGHEST
RING = 8


def tn(left, right, precision=EXACT):
    return lax.dot_general(
        left, right, (((0,), (0,)), ((), ())), precision=precision, preferred_element_type=F32
    )


def nn(left, right, precision=EXACT):
    return lax.dot_general(
        left, right, (((1,), (0,)), ((), ())), precision=precision, preferred_element_type=F32
    )


def nt(left, right, precision=EXACT):
    return lax.dot_general(
        left, right, (((1,), (1,)), ((), ())), precision=precision, preferred_element_type=F32
    )


def split_tn(piece, wide):
    def thirds(value):
        first = value.astype(BF16).astype(F32)
        rest = value - first
        second = rest.astype(BF16).astype(F32)
        return first, second, rest - second

    a1, a2, a3 = thirds(piece)
    b1, b2, b3 = thirds(wide)
    left = jnp.concatenate([a1, a1, a2, a1, a2, a3], 0).astype(BF16)
    right = jnp.concatenate([b1, b2, b1, b3, b2, b1], 0).astype(BF16)
    return tn(left, right, None)


def eliminate_panel(work, first, count, panel):
    depth = 8
    start = depth * panel
    group = pl.ds(first, count)
    row_at = lax.broadcasted_iota(jnp.int32, (count, depth, 128), 1)
    rows = work[group, start : start + depth, :]
    columns = [
        jnp.broadcast_to(rows[:, :, start + j : start + j + 1], (count, depth, 128))
        for j in range(depth)
    ]
    scale = jnp.zeros((count, depth, 128), F32)
    for j in range(depth):
        column = columns[j]
        pivot = jnp.broadcast_to(column[:, j : j + 1, :], (count, depth, 128))
        scale = jnp.where(row_at == j, lax.rsqrt(pivot), scale)
        if j < depth - 1:
            share = jnp.where(row_at > j, column / pivot, 0.0)
            rows = rows - share * rows[:, j : j + 1, :]
            for k in range(j + 1, depth):
                columns[k] = columns[k] - share * columns[k][:, j : j + 1, :]
    done = rows * scale
    work[group, start : start + depth, :] = done
    after = start + depth
    if after < 64:
        for n in range(count):
            update = split_tn(done[n][:, :64], done[n])
            work[first + n, after:, :] = work[first + n, after:, :] - update[after:, :]


def kernel(
    bases,
    leaf_transfer,
    top_transfer,
    couplings,
    top_couplings,
    coupling_target,
    coupling_dest,
    coupling_local,
    top_target,
    top_source,
    leaf_bases,
    leaf_transfers,
    top_transfers,
    new_couplings,
    new_top,
    work,
    h_mine,
    h_theirs,
    k_mine,
    k_theirs,
    table,
    top_table,
    stacked,
    blocks,
    halves,
    pair_sem,
    a_send,
    a_recv,
    b_send,
    b_recv,
    s_send,
    s_recv,
    ta_send,
    ta_recv,
    tb_send,
    tb_recv,
    ts_send,
    ts_recv,
):
    me = lax.axis_index("leaf")
    near = lax.axis_index("near")
    core = me % 2
    y = (me // 2) % RING
    z = me // (2 * RING)
    a = z + core * (y - z)
    b = y + core * (z - y)

    def device(a_at, b_at):
        first = a_at + core * (b_at - a_at)
        second = b_at + core * (a_at - b_at)
        return {"leaf": (first * RING + second) * 2 + core}

    def wrap(value):
        return (value + 2 * RING) % RING

    a_right, a_left = device(wrap(a + 1), b), device(wrap(a - 1), b)
    b_right, b_left = device(a, wrap(b + 1)), device(a, wrap(b - 1))
    sibling = {"leaf": me + 1 - 2 * core}
    cousin = {"leaf": me + 2 - 4 * ((me // 2) % 2)}
    parity = core
    upper = (me // 2) % 2

    barrier = pltpu.get_barrier_semaphore()
    for neighbour in (a_right, a_left, b_right, b_left, sibling):
        pl.semaphore_signal(barrier, inc=1, device_id=neighbour, device_id_type=MESH)
    pl.semaphore_wait(barrier, 5)

    def remote(source, target, send, recv, to):
        return pltpu.make_async_remote_copy(
            src_ref=source,
            dst_ref=target,
            send_sem=send,
            recv_sem=recv,
            device_id=to,
            device_id_type=MESH,
        )

    def row_of(b_at, a_at):
        return core * 64 + b_at * RING + a_at

    def leaf_span(b_at, a_at, low, high):
        return table.at[pl.ds(row_of(b_at, a_at) * 4 + low, high - low)]

    started = []

    def go(copy):
        copy.start()
        started.append(copy)

    row = lax.broadcasted_iota(jnp.int32, (64, 128), 0)
    lane = lax.broadcasted_iota(jnp.int32, (64, 128), 1)
    keep = row <= lane % 64
    low_lane = lane < 64
    unit = jnp.where(row == lane - 64, 1.0, 0.0)

    for n in range(20):
        work[n] = unit
    for n in range(8):
        gram = tn(bases[n], bases[n])
        work[n, :, 0:64] = gram
        h_mine[n] = tn(leaf_transfer[n], nn(gram, leaf_transfer[n]))
    to_sibling = remote(h_mine, h_theirs, pair_sem.at[0], pair_sem.at[1], sibling)
    to_sibling.start()

    for panel in range(4):
        eliminate_panel(work, 0, 8, panel)

    to_sibling.wait()
    for n in range(8):
        work[8 + n, :, 0:64] = h_mine[n] + h_theirs[n]
    for n in range(4):
        mid = work[8 + parity * 4 + n][:, 0:64]
        k_mine[n] = tn(top_transfer[n], nn(mid, top_transfer[n]))
    to_cousin = remote(k_mine, k_theirs, pair_sem.at[2], pair_sem.at[3], cousin)
    to_cousin.start()

    for panel in range(4, 8):
        eliminate_panel(work, 0, 8, panel)

    def pair_of(first, second):
        both = jnp.where(low_lane, first, pltpu.roll(second, 64, 1))
        return jnp.where(keep, both, 0.0).astype(BF16)

    for q in range(4):
        table[row_of(b, a) * 4 + q] = pair_of(work[2 * q], work[2 * q + 1])

    def a_copy(k, way):
        at = wrap(a - way * k)
        low, high = (0, 4) if k < 3 else ((0, 2) if way > 0 else (2, 4))
        lane_at = k if way > 0 else 4 + k
        return remote(
            leaf_span(b, at, low, high),
            leaf_span(b, at, low, high),
            a_send.at[lane_at],
            a_recv.at[lane_at],
            a_right if way > 0 else a_left,
        )

    def a_arrival(k, way):
        at = wrap(a - way * k)
        low, high = (0, 4) if k < 4 else ((0, 2) if way > 0 else (2, 4))
        lane_at = k - 1 if way > 0 else 3 + k
        span = leaf_span(b, at, low, high)
        return remote(span, span, a_send.at[lane_at], a_recv.at[lane_at], sibling)

    offsets = [0, 1, -1, 2, -2, 3, -3, 4]

    def b_copy(h, w, way):
        b_at, a_at = wrap(b - way * h), wrap(a - offsets[w])
        low, high = (0, 4) if h < 3 else ((0, 2) if way > 0 else (2, 4))
        span = leaf_span(b_at, a_at, low, high)
        lane_at = (h if way > 0 else 4 + h) * 8 + w
        return remote(
            span, span, b_send.at[lane_at], b_recv.at[lane_at], b_right if way > 0 else b_left
        )

    def b_arrival(h, w, way):
        b_at, a_at = wrap(b - way * h), wrap(a - offsets[w])
        low, high = (0, 4) if h < 4 else ((0, 2) if way > 0 else (2, 4))
        span = leaf_span(b_at, a_at, low, high)
        lane_at = (h - 1 if way > 0 else 3 + h) * 8 + w
        return remote(span, span, b_send.at[lane_at], b_recv.at[lane_at], sibling)

    def s_copy(b_at, slot):
        span = table.at[pl.ds(row_of(b_at, 0) * 4, 32)]
        return remote(span, span, s_send.at[slot], s_recv.at[slot], sibling)

    def s_arrival(b_offset, slot):
        at = wrap(a + b_offset)
        span = table.at[pl.ds(((1 - core) * 64 + at * RING) * 4, 32)]
        return remote(span, span, s_send.at[slot], s_recv.at[slot], sibling)

    b_offsets = [0, -1, 1, -2, 2, -3, 3, 4]

    def leaf_event(h, w):
        if h == 0:
            if w == 0:
                go(a_copy(0, 1))
                go(a_copy(0, -1))
            elif w < 7:
                way = 1 if offsets[w] > 0 else -1
                k = abs(offsets[w])
                a_arrival(k, way).wait_recv()
                go(a_copy(k, way))
            else:
                a_arrival(4, 1).wait_recv()
                a_arrival(4, -1).wait_recv()
            go(b_copy(0, w, 1))
            go(b_copy(0, w, -1))
        else:
            b_arrival(h, w, 1).wait_recv()
            b_arrival(h, w, -1).wait_recv()
            if h < 4:
                go(b_copy(h, w, 1))
                go(b_copy(h, w, -1))
        if w == 7:
            for slot, offset in enumerate(b_offsets):
                if abs(offset) == h:
                    go(s_copy(wrap(b + offset), slot))

    def top_a_copy(k, way):
        at = wrap(a - way * k)
        lane_at = k if way > 0 else 4 + k
        span = top_table.at[row_of(b, at)]
        return remote(
            span, span, ta_send.at[lane_at], ta_recv.at[lane_at], a_right if way > 0 else a_left
        )

    def top_a_arrival(k, way):
        at = wrap(a - way * k)
        lane_at = k - 1 if way > 0 else 3 + k
        span = top_table.at[row_of(b, at)]
        return remote(span, span, ta_send.at[lane_at], ta_recv.at[lane_at], sibling)

    def top_b_span(b_at, h, way):
        low, size = (0, 8) if h < 4 else ((0, 4) if way > 0 else (4, 4))
        return top_table.at[pl.ds(row_of(b_at, 0) + low, size)]

    def top_b_copy(h, way):
        span = top_b_span(wrap(b - way * h), h + 1, way)
        lane_at = h if way > 0 else 4 + h
        return remote(
            span, span, tb_send.at[lane_at], tb_recv.at[lane_at], b_right if way > 0 else b_left
        )

    def top_b_arrival(h, way):
        span = top_b_span(wrap(b - way * h), h, way)
        lane_at = h - 1 if way > 0 else 3 + h
        return remote(span, span, tb_send.at[lane_at], tb_recv.at[lane_at], sibling)

    def top_s_copy(b_at, slot):
        span = top_table.at[pl.ds(row_of(b_at, 0), 8)]
        return remote(span, span, ts_send.at[slot], ts_recv.at[slot], sibling)

    def top_s_arrival(b_offset, slot):
        at = wrap(a + b_offset)
        span = top_table.at[pl.ds((1 - core) * 64 + at * RING, 8)]
        return remote(span, span, ts_send.at[slot], ts_recv.at[slot], sibling)

    def top_first():
        first = work[16 + upper * 2]
        second = work[17 + upper * 2]
        top_table[row_of(b, a)] = pair_of(first, second)
        go(top_a_copy(0, 1))
        go(top_a_copy(0, -1))

    def top_along_a(k):
        top_a_arrival(k, 1).wait_recv()
        if k < 4:
            top_a_arrival(k, -1).wait_recv()
            go(top_a_copy(k, 1))
            if k < 3:
                go(top_a_copy(k, -1))

    def top_along_b(h):
        if h > 0:
            top_b_arrival(h, 1).wait_recv()
            top_b_arrival(h, -1).wait_recv()
        if h < 4:
            go(top_b_copy(h, 1))
            go(top_b_copy(h, -1))
        for slot, offset in enumerate(b_offsets):
            if abs(offset) == h:
                go(top_s_copy(wrap(b + offset), slot))

    top_events = (
        [top_first]
        + [functools.partial(top_along_a, k) for k in range(1, 5)]
        + [functools.partial(top_along_b, h) for h in range(5)]
    )

    def top_gram():
        to_cousin.wait()
        for n in range(4):
            work[16 + n, :, 0:64] = k_mine[n] + k_theirs[n]

    def factor(n):
        return jnp.where(keep, work[n], 0.0)[:, 0:64]

    def inverse_transposed(n):
        return work[n][:, 64:128]

    def finish_bases():
        for k in range(2):
            at = near * 2 + k
            leaf_bases[k] = nt(bases[at], inverse_transposed(at))

    def finish_leaf(n):
        piece = nn(factor(n), leaf_transfer[n])
        leaf_transfers[n] = nt(piece, inverse_transposed(8 + n))

    def finish_top(n):
        piece = nn(factor(8 + parity * 4 + n), top_transfer[n])
        top_transfers[n] = nt(piece, inverse_transposed(16 + n))

    def stack_factors():
        for n in range(8):
            low = factor(n).astype(BF16)
            stacked[n] = jnp.concatenate([low[:, :32], low[:, 32:]], 0)

    def unpack_blocks(first, last):
        for k in range(first, last):
            slab = jnp.concatenate(
                [couplings[k].astype(F32), couplings[k + 32].astype(F32)], 0
            )
            blocks[pl.ds(k, 128, stride=32), :] = jnp.transpose(slab)

    def half_step(first, last):
        for n in range(first, last):
            block = blocks[32 * n : 32 * n + 32, :].astype(BF16)
            both = nn(stacked[coupling_target[n]], block, None)
            mixed = jnp.where(low_lane, both[0:64], both[64:128])
            mixed = mixed + pltpu.roll(mixed, 64, 1)
            odd = coupling_local[n] & 1
            here = (lane // 64) == odd
            halves[n] = jnp.where(here, mixed, 0.0).astype(BF16)

    tasks = [top_gram]
    tasks += [functools.partial(eliminate_panel, work, 8, 12, panel) for panel in range(8)]
    late = [stack_factors, finish_bases]
    late += [functools.partial(unpack_blocks, k, k + 4) for k in range(0, 32, 4)]
    late += [functools.partial(half_step, n, n + 16) for n in range(0, 128, 16)]
    late += [functools.partial(finish_leaf, n) for n in range(8)]
    late += [functools.partial(finish_top, n) for n in range(4)]

    events = [functools.partial(leaf_event, h, w) for h in range(5) for w in range(8)]
    tops_at = {9: 0, 12: 1, 15: 2, 18: 3, 21: 4, 22: 5, 26: 6, 30: 7, 34: 8, 39: 9}
    queue = tasks + late
    for place, event in enumerate(events):
        event()
        if place in tops_at:
            top_events[tops_at[place]]()
        if queue:
            queue.pop(0)()
    while queue:
        queue.pop(0)()

    for slot, offset in enumerate(b_offsets):
        top_s_arrival(offset, slot).wait_recv()
        s_arrival(offset, slot).wait_recv()

    def table_row(leaf_place):
        c = leaf_place & 1
        y_at = (leaf_place >> 1) & 7
        z_at = leaf_place >> 4
        return c * 64 + (y_at + c * (z_at - y_at)) * RING + z_at + c * (y_at - z_at)

    quad = me // 4

    def top_tile(cluster):
        place = (cluster >> 3) * 4 + (cluster & 2) + ((cluster >> 2) & 1)
        return top_table[table_row(place)]

    for n in range(16):
        target = quad * 8 + top_target[n]
        source = top_source[n]
        left = jnp.where((lane // 64) == (target & 1), top_tile(target), jnp.zeros((), BF16))
        block = top_couplings[n]
        double = jnp.concatenate([block, block], 1)
        half = nn(left, jnp.concatenate([double, double], 0), None)
        half = jnp.where((lane // 64) == (source & 1), half, 0.0).astype(BF16)
        new_top[n] = nt(half, top_tile(source), None).astype(BF16)

    for n in range(128):
        place = table_row(coupling_dest[n]) * 4 + (coupling_local[n] >> 1)
        new = nt(halves[n], table[place], None)
        blocks[32 * n : 32 * n + 32, :] = jnp.concatenate([new[0:32], new[32:64]], 1)
    for k in range(32):
        slab = jnp.transpose(blocks[pl.ds(k, 128, stride=32), :]).astype(BF16)
        new_couplings[k] = slab[0:64]
        new_couplings[k + 32] = slab[64:128]

    for copy in started:
        copy.wait_send()


def on_device(
    bases,
    leaf_transfer,
    top_transfer,
    couplings,
    coupling_target,
    coupling_dest,
    coupling_local,
    top_couplings,
    top_target,
    top_source,
):
    vmem = pl.BlockSpec(memory_space=pltpu.VMEM)
    smem = pl.BlockSpec(memory_space=pltpu.SMEM)
    dma = pltpu.SemaphoreType.DMA
    leaf_bases, leaf_transfers, top_transfers, new_couplings, new_top = pl.pallas_call(
        kernel,
        out_shape=(
            jax.ShapeDtypeStruct((2, 64, 64), F32),
            jax.ShapeDtypeStruct((8, 64, 64), F32),
            jax.ShapeDtypeStruct((4, 64, 64), F32),
            jax.ShapeDtypeStruct((64, 64, 128), BF16),
            jax.ShapeDtypeStruct((16, 64, 64), BF16),
        ),
        in_specs=[vmem] * 5 + [smem] * 5,
        out_specs=[vmem] * 5,
        scratch_shapes=[
            pltpu.VMEM((20, 64, 128), F32),
            pltpu.VMEM((8, 64, 64), F32),
            pltpu.VMEM((8, 64, 64), F32),
            pltpu.VMEM((4, 64, 64), F32),
            pltpu.VMEM((4, 64, 64), F32),
            pltpu.VMEM((512, 64, 128), BF16),
            pltpu.VMEM((128, 64, 128), BF16),
            pltpu.VMEM((8, 128, 32), BF16),
            pltpu.VMEM((4096, 128), F32),
            pltpu.VMEM((128, 64, 128), BF16),
            dma((4,)),
            dma((8,)),
            dma((8,)),
            dma((64,)),
            dma((64,)),
            dma((8,)),
            dma((8,)),
            dma((8,)),
            dma((8,)),
            dma((8,)),
            dma((8,)),
            dma((8,)),
            dma((8,)),
        ],
        compiler_params=pltpu.CompilerParams(
            collective_id=0, has_side_effects=True, vmem_limit_bytes=40 * 2**20
        ),
    )(
        bases,
        leaf_transfer,
        top_transfer,
        jnp.transpose(couplings, (1, 2, 0)),
        top_couplings,
        coupling_target,
        coupling_dest[:, 0],
        coupling_local,
        top_target,
        top_source,
    )
    return (
        leaf_bases,
        leaf_transfers,
        top_transfers,
        jnp.transpose(new_couplings, (2, 0, 1)),
        new_top,
    )


def solution(mesh):
    in_specs = (
        P("leaf", None, None),
        P("leaf", None, None),
        P("leaf", None, None),
        P(("leaf", "near"), None, None),
        P(("leaf", "near")),
        P(("leaf", "near"), None),
        P(("leaf", "near")),
        P(("leaf", "near"), None, None),
        P(("leaf", "near")),
        P(("leaf", "near")),
    )
    out_specs = (
        P(("leaf", "near"), None, None),
        P("leaf", None, None),
        P("leaf", None, None),
        P(("leaf", "near"), None, None),
        P(("leaf", "near"), None, None),
    )
    return jax.shard_map(
        on_device, mesh=mesh, in_specs=in_specs, out_specs=out_specs, check_vma=False
    )
```

```python
import functools

import jax
import jax.numpy as jnp
from jax import lax
from jax.experimental import pallas as pl
from jax.experimental.pallas import tpu as pltpu
from jax.sharding import PartitionSpec as P

MESH = pl.DeviceIdType.MESH
F32 = jnp.float32
BF16 = jnp.bfloat16
EXACT = lax.Precision.HIGHEST
RING = 8


def tn(left, right, precision=EXACT):
    return lax.dot_general(
        left, right, (((0,), (0,)), ((), ())), precision=precision, preferred_element_type=F32
    )


def nn(left, right, precision=EXACT):
    return lax.dot_general(
        left, right, (((1,), (0,)), ((), ())), precision=precision, preferred_element_type=F32
    )


def nt(left, right, precision=EXACT):
    return lax.dot_general(
        left, right, (((1,), (1,)), ((), ())), precision=precision, preferred_element_type=F32
    )


def split_tn(piece, wide):
    def thirds(value):
        first = value.astype(BF16).astype(F32)
        rest = value - first
        second = rest.astype(BF16).astype(F32)
        return first, second, rest - second

    a1, a2, a3 = thirds(piece)
    b1, b2, b3 = thirds(wide)
    left = jnp.concatenate([a1, a1, a2, a1, a2, a3], 0).astype(BF16)
    right = jnp.concatenate([b1, b2, b1, b3, b2, b1], 0).astype(BF16)
    return tn(left, right, None)


def eliminate_panel(work, first, count, panel):
    depth = 8
    start = depth * panel
    group = pl.ds(first, count)
    row_at = lax.broadcasted_iota(jnp.int32, (count, depth, 128), 1)
    rows = work[group, start : start + depth, :]
    columns = [
        jnp.broadcast_to(rows[:, :, start + j : start + j + 1], (count, depth, 128))
        for j in range(depth)
    ]
    scale = jnp.zeros((count, depth, 128), F32)
    for j in range(depth):
        column = columns[j]
        pivot = jnp.broadcast_to(column[:, j : j + 1, :], (count, depth, 128))
        scale = jnp.where(row_at == j, lax.rsqrt(pivot), scale)
        if j < depth - 1:
            share = jnp.where(row_at > j, column / pivot, 0.0)
            rows = rows - share * rows[:, j : j + 1, :]
            for k in range(j + 1, depth):
                columns[k] = columns[k] - share * columns[k][:, j : j + 1, :]
    done = rows * scale
    work[group, start : start + depth, :] = done
    after = start + depth
    if after < 64:
        for n in range(count):
            update = split_tn(done[n][:, :64], done[n])
            work[first + n, after:, :] = work[first + n, after:, :] - update[after:, :]


def kernel(
    bases_in,
    leaf_transfer_in,
    top_transfer_in,
    couplings_in,
    top_couplings_in,
    coupling_target_in,
    coupling_dest_in,
    coupling_local_in,
    top_target_in,
    top_source_in,
    leaf_bases,
    leaf_transfers,
    top_transfers,
    new_couplings,
    new_top,
    bases,
    leaf_transfer,
    top_transfer,
    couplings,
    top_couplings,
    coupling_target,
    coupling_dest,
    coupling_local,
    top_target,
    top_source,
    work,
    h_mine,
    h_theirs,
    k_mine,
    k_theirs,
    table,
    top_table,
    stacked,
    blocks,
    halves,
    in_sem,
    pair_sem,
    a_send,
    a_recv,
    ta_send,
    ta_recv,
    b_send,
    b_recv,
    s_send,
    s_recv,
):
    loads = [
        pltpu.make_async_copy(source, target, in_sem.at[n])
        for n, (source, target) in enumerate(
            [
                (bases_in, bases),
                (leaf_transfer_in, leaf_transfer),
                (top_transfer_in, top_transfer),
                (couplings_in, couplings),
                (top_couplings_in, top_couplings),
                (coupling_target_in, coupling_target),
                (coupling_dest_in, coupling_dest),
                (coupling_local_in, coupling_local),
                (top_target_in, top_target),
                (top_source_in, top_source),
            ]
        )
    ]
    for copy in loads:
        copy.start()

    me = lax.axis_index("leaf")
    near = lax.axis_index("near")
    core = me % 2
    y = (me // 2) % RING
    z = me // (2 * RING)
    a = z + core * (y - z)
    b = y + core * (z - y)

    def device(a_at, b_at):
        first = a_at + core * (b_at - a_at)
        second = b_at + core * (a_at - b_at)
        return {"leaf": (first * RING + second) * 2 + core}

    def wrap(value):
        return (value + 2 * RING) % RING

    b_right, b_left = device(a, wrap(b + 1)), device(a, wrap(b - 1))
    sibling = {"leaf": me + 1 - 2 * core}
    cousin = {"leaf": me + 2 - 4 * ((me // 2) % 2)}
    parity = core
    upper = (me // 2) % 2

    barrier = pltpu.get_barrier_semaphore()
    partners = [sibling, b_right, b_left] + [device(wrap(a + k), b) for k in range(1, RING)]
    for partner in partners:
        pl.semaphore_signal(barrier, inc=1, device_id=partner, device_id_type=MESH)
    pl.semaphore_wait(barrier, len(partners))

    def remote(source, target, send, recv, to):
        return pltpu.make_async_remote_copy(
            src_ref=source,
            dst_ref=target,
            send_sem=send,
            recv_sem=recv,
            device_id=to,
            device_id_type=MESH,
        )

    def row_of(b_at, a_at):
        return core * 64 + b_at * RING + a_at

    started = []

    def go(copy):
        copy.start()
        started.append(copy)

    row = lax.broadcasted_iota(jnp.int32, (64, 128), 0)
    lane = lax.broadcasted_iota(jnp.int32, (64, 128), 1)
    keep = row <= lane % 64
    low_lane = lane < 64
    unit = jnp.where(row == lane - 64, 1.0, 0.0)
    row32 = lax.broadcasted_iota(jnp.int32, (32, 128), 0)
    lane32 = lax.broadcasted_iota(jnp.int32, (32, 128), 1)

    for n in range(20):
        work[n] = unit
    loads[0].wait()
    loads[1].wait()
    for n in range(8):
        gram = tn(bases[n], bases[n])
        work[n, :, 0:64] = gram
        h_mine[n] = tn(leaf_transfer[n], nn(gram, leaf_transfer[n]))
    to_sibling = remote(h_mine, h_theirs, pair_sem.at[0], pair_sem.at[1], sibling)
    to_sibling.start()

    for panel in range(4):
        eliminate_panel(work, 0, 8, panel)

    to_sibling.wait()
    loads[2].wait()
    for n in range(8):
        work[8 + n, :, 0:64] = h_mine[n] + h_theirs[n]
    for n in range(4):
        mid = work[8 + parity * 4 + n][:, 0:64]
        k_mine[n] = tn(top_transfer[n], nn(mid, top_transfer[n]))
    to_cousin = remote(k_mine, k_theirs, pair_sem.at[2], pair_sem.at[3], cousin)
    to_cousin.start()

    for panel in range(4, 8):
        eliminate_panel(work, 0, 8, panel)

    def pair_of(first, second):
        both = jnp.where(low_lane, first, pltpu.roll(second, 64, 1))
        return jnp.where(keep, both, 0.0).astype(BF16)

    for g in range(2):
        f0, f1, f2, f3 = (work[4 * g + i] for i in range(4))
        tile = row_of(b, a) * 6 + 3 * g
        table[tile] = pair_of(f0, f1)[0:32]
        table[tile + 1] = pair_of(f2, f3)[0:32]
        corner = jnp.where(
            lane32 < 64,
            jnp.where(lane32 < 32, pltpu.roll(f0[32:64], 96, 1), f1[32:64]),
            jnp.where(lane32 < 96, pltpu.roll(f2[32:64], 32, 1), pltpu.roll(f3[32:64], 64, 1)),
        )
        table[tile + 2] = jnp.where(row32 <= lane32 % 32, corner, 0.0).astype(BF16)

    def own_sends(span, send, recv):
        for k in (4, 3, 5, 2, 6, 1, 7):
            go(remote(span, span, send.at[k], recv.at[k], device(wrap(a + k), b)))

    def own_arrivals(span_of, send, recv):
        for k in range(1, RING):
            span = span_of(wrap(a - k))
            remote(span, span, send.at[k], recv.at[k], sibling).wait_recv()

    def leaf_item(a_at):
        return table.at[pl.ds(row_of(b, a_at) * 6, 6)]

    def top_item(a_at):
        return top_table.at[row_of(b, a_at)]

    def span_at(place, piece, part=None):
        if piece < 2:
            return table.at[pl.ds((place + 4 * piece) * 6, 24)]
        low, size = (0, 8) if part is None else (4 * part, 4)
        return top_table.at[pl.ds(place + low, size)]

    def carried(h, piece, way):
        return h < 4 or piece == 2 or piece == (0 if way > 0 else 1)

    def b_span(h, piece, way):
        part = None if h < 4 else (0 if way > 0 else 1)
        return span_at(row_of(wrap(b - way * h), 0), piece, part)

    def b_slot(h, piece, way):
        return ((h - 1) * 2 + (way > 0)) * 3 + piece

    def forward(h, piece):
        for way in (1, -1):
            if carried(h + 1, piece, way):
                place = row_of(wrap(b - way * h), 0)
                part = None if h + 1 < 4 else (0 if way > 0 else 1)
                span = span_at(place, piece, part)
                slot = b_slot(h + 1, piece, way)
                to = b_right if way > 0 else b_left
                go(remote(span, span, b_send.at[slot], b_recv.at[slot], to))

    def arrive(h, piece):
        for way in (1, -1):
            if carried(h, piece, way):
                span = b_span(h, piece, way)
                slot = b_slot(h, piece, way)
                remote(span, span, b_send.at[slot], b_recv.at[slot], sibling).wait_recv()

    b_offsets = [0, -1, 1, -2, 2, -3, 3, 4]

    def hand_over(h, piece):
        for slot, offset in enumerate(b_offsets):
            if abs(offset) == h:
                span = span_at(row_of(wrap(b + offset), 0), piece)
                at = slot * 3 + piece
                go(remote(span, span, s_send.at[at], s_recv.at[at], sibling))

    def handed(piece):
        for slot, offset in enumerate(b_offsets):
            span = span_at((1 - core) * 64 + wrap(a + offset) * RING, piece)
            at = slot * 3 + piece
            remote(span, span, s_send.at[at], s_recv.at[at], sibling).wait_recv()

    def second_ring(h, piece):
        if h > 0:
            arrive(h, piece)
        if h < 4:
            forward(h, piece)
        hand_over(h, piece)

    def factor(n):
        return jnp.where(keep, work[n], 0.0)[:, 0:64]

    def inverse_transposed(n):
        return work[n][:, 64:128]

    def finish_bases():
        for k in range(2):
            at = near * 2 + k
            leaf_bases[k] = nt(bases[at], inverse_transposed(at))

    def finish_leaf(n):
        piece = nn(factor(n), leaf_transfer[n])
        leaf_transfers[n] = nt(piece, inverse_transposed(8 + n))

    def finish_top(n):
        piece = nn(factor(8 + parity * 4 + n), top_transfer[n])
        top_transfers[n] = nt(piece, inverse_transposed(16 + n))

    def stack_factors():
        for n in range(8):
            low = factor(n).astype(BF16)
            stacked[n] = jnp.concatenate([low[:, :32], low[:, 32:]], 0)

    def unpack_blocks(first, last):
        for k in range(first, last):
            slab = jnp.concatenate([couplings[k].astype(F32), couplings[k + 32].astype(F32)], 0)
            blocks[pl.ds(k, 128, stride=32), :] = jnp.transpose(slab)

    def half_step(first, last):
        for n in range(first, last):
            block = blocks[32 * n : 32 * n + 32, :].astype(BF16)
            both = nn(stacked[coupling_target[n]], block, None)
            mixed = jnp.where(low_lane, both[0:64], both[64:128])
            mixed = mixed + pltpu.roll(mixed, 64, 1)
            right = jnp.where((lane // 32) % 2 == 1, mixed, pltpu.roll(mixed, 32, 1))
            local = coupling_local[n] & 3
            mixed = jnp.where(lane // 64 == (local & 1), mixed, 0.0)
            right = jnp.where(lane // 32 == local, right, 0.0)
            halves[n, :, 0:128] = mixed.astype(BF16)
            halves[n, :, 128:256] = right.astype(BF16)

    own_sends(leaf_item(a), a_send, a_recv)

    to_cousin.wait()
    for n in range(4):
        work[16 + n, :, 0:64] = k_mine[n] + k_theirs[n]
    for panel in range(8):
        eliminate_panel(work, 8, 12, panel)
        if panel == 5:
            own_arrivals(leaf_item, a_send, a_recv)
            second_ring(0, 0)
            second_ring(0, 1)

    top_table[row_of(b, a)] = pair_of(work[16 + upper * 2], work[17 + upper * 2])
    own_sends(top_item(a), ta_send, ta_recv)

    for copy in loads[3:]:
        copy.wait()
    stack_factors()

    queue = [functools.partial(unpack_blocks, k, k + 8) for k in range(0, 32, 8)]
    queue += [functools.partial(half_step, n, n + 32) for n in range(0, 128, 32)]
    queue += [finish_bases]
    queue += [functools.partial(finish_leaf, n) for n in range(8)]
    queue += [functools.partial(finish_top, n) for n in range(4)]

    def top_hop_zero():
        own_arrivals(top_item, ta_send, ta_recv)
        second_ring(0, 2)

    events = [functools.partial(second_ring, 1, 0), functools.partial(second_ring, 1, 1), top_hop_zero]
    for h in range(2, 5):
        events += [functools.partial(second_ring, h, 0), functools.partial(second_ring, h, 1)]
        events += [functools.partial(second_ring, h - 1, 2)]
    events += [functools.partial(second_ring, 4, 2)]
    for event in events:
        event()
        for _ in range(2):
            if queue:
                queue.pop(0)()
    while queue:
        queue.pop(0)()

    handed(0)
    handed(1)

    def table_row(leaf_place):
        c = leaf_place & 1
        y_at = (leaf_place >> 1) & 7
        z_at = leaf_place >> 4
        return c * 64 + (y_at + c * (z_at - y_at)) * RING + z_at + c * (y_at - z_at)

    empty = jnp.zeros((32, 128), BF16)
    for n in range(128):
        local = coupling_local[n]
        tile = table_row(coupling_dest[n]) * 6 + (local >> 2) * 3
        upper_rows = jnp.concatenate([table[tile + ((local >> 1) & 1)], empty], 1)
        lower_rows = jnp.concatenate([empty, table[tile + 2]], 1)
        new = nt(halves[n], jnp.concatenate([upper_rows, lower_rows], 0), None)
        blocks[32 * n : 32 * n + 32, :] = jnp.concatenate([new[0:32], new[32:64]], 1)
    for k in range(32):
        slab = jnp.transpose(blocks[pl.ds(k, 128, stride=32), :]).astype(BF16)
        new_couplings[k] = slab[0:64]
        new_couplings[k + 32] = slab[64:128]

    handed(2)
    quad = me // 4

    def top_tile(cluster):
        place = (cluster >> 3) * 4 + (cluster & 2) + ((cluster >> 2) & 1)
        return top_table[table_row(place)]

    for n in range(16):
        target = quad * 8 + top_target[n]
        source = top_source[n]
        left = jnp.where((lane // 64) == (target & 1), top_tile(target), jnp.zeros((), BF16))
        block = top_couplings[n]
        double = jnp.concatenate([block, block], 1)
        half = nn(left, jnp.concatenate([double, double], 0), None)
        half = jnp.where((lane // 64) == (source & 1), half, 0.0).astype(BF16)
        new_top[n] = nt(half, top_tile(source), None).astype(BF16)

    for copy in started:
        copy.wait_send()


def hand_out(*refs):
    count = len(refs) // 2
    sems = refs[-1]
    copies = [
        pltpu.make_async_copy(refs[n], refs[count + n], sems.at[n]) for n in range(count)
    ]
    for copy in copies:
        copy.start()
    for copy in copies:
        copy.wait()


def on_device(
    bases,
    leaf_transfer,
    top_transfer,
    couplings,
    coupling_target,
    coupling_dest,
    coupling_local,
    top_couplings,
    top_target,
    top_source,
):
    vmem = pl.BlockSpec(memory_space=pltpu.VMEM)
    anywhere = pl.BlockSpec(memory_space=pl.ANY)
    dma = pltpu.SemaphoreType.DMA
    shapes = (
        jax.ShapeDtypeStruct((2, 64, 64), F32),
        jax.ShapeDtypeStruct((8, 64, 64), F32),
        jax.ShapeDtypeStruct((4, 64, 64), F32),
        jax.ShapeDtypeStruct((64, 64, 128), BF16),
        jax.ShapeDtypeStruct((16, 64, 64), BF16),
    )
    results = pl.pallas_call(
        kernel,
        out_shape=shapes,
        in_specs=[anywhere] * 10,
        out_specs=[vmem] * 5,
        scratch_shapes=[
            pltpu.VMEM((8, 64, 64), F32),
            pltpu.VMEM((8, 64, 64), F32),
            pltpu.VMEM((4, 64, 64), F32),
            pltpu.VMEM((64, 64, 128), BF16),
            pltpu.VMEM((16, 64, 64), BF16),
            pltpu.SMEM((128,), jnp.int32),
            pltpu.SMEM((128,), jnp.int32),
            pltpu.SMEM((128,), jnp.int32),
            pltpu.SMEM((16,), jnp.int32),
            pltpu.SMEM((16,), jnp.int32),
            pltpu.VMEM((20, 64, 128), F32),
            pltpu.VMEM((8, 64, 64), F32),
            pltpu.VMEM((8, 64, 64), F32),
            pltpu.VMEM((4, 64, 64), F32),
            pltpu.VMEM((4, 64, 64), F32),
            pltpu.VMEM((768, 32, 128), BF16),
            pltpu.VMEM((128, 64, 128), BF16),
            pltpu.VMEM((8, 128, 32), BF16),
            pltpu.VMEM((4096, 128), F32),
            pltpu.VMEM((128, 64, 256), BF16),
            dma((10,)),
            dma((4,)),
            dma((8,)),
            dma((8,)),
            dma((8,)),
            dma((8,)),
            dma((24,)),
            dma((24,)),
            dma((24,)),
            dma((24,)),
        ],
        compiler_params=pltpu.CompilerParams(
            collective_id=0, has_side_effects=True, vmem_limit_bytes=58 * 2**20
        ),
    )(
        bases,
        leaf_transfer,
        top_transfer,
        jnp.transpose(couplings, (1, 2, 0)),
        top_couplings,
        coupling_target,
        coupling_dest[:, 0],
        coupling_local,
        top_target,
        top_source,
    )
    leaf_bases, leaf_transfers, top_transfers, new_couplings, new_top = pl.pallas_call(
        hand_out,
        out_shape=shapes,
        in_specs=[anywhere] * 5,
        out_specs=[anywhere] * 5,
        scratch_shapes=[dma((5,))],
    )(*results)
    return (
        leaf_bases,
        leaf_transfers,
        top_transfers,
        jnp.transpose(new_couplings, (2, 0, 1)),
        new_top,
    )


def solution(mesh):
    in_specs = (
        P("leaf", None, None),
        P("leaf", None, None),
        P("leaf", None, None),
        P(("leaf", "near"), None, None),
        P(("leaf", "near")),
        P(("leaf", "near"), None),
        P(("leaf", "near")),
        P(("leaf", "near"), None, None),
        P(("leaf", "near")),
        P(("leaf", "near")),
    )
    out_specs = (
        P(("leaf", "near"), None, None),
        P("leaf", None, None),
        P("leaf", None, None),
        P(("leaf", "near"), None, None),
        P(("leaf", "near"), None, None),
    )
    return jax.shard_map(
        on_device, mesh=mesh, in_specs=in_specs, out_specs=out_specs, check_vma=False
    )
```

```python
import functools

import jax
import jax.numpy as jnp
from jax import lax
from jax.experimental import pallas as pl
from jax.experimental.pallas import tpu as pltpu
from jax.sharding import PartitionSpec as P

MESH = pl.DeviceIdType.MESH
F32 = jnp.float32
BF16 = jnp.bfloat16
EXACT = lax.Precision.HIGHEST
RING = 8


def tn(left, right, precision=EXACT):
    return lax.dot_general(
        left, right, (((0,), (0,)), ((), ())), precision=precision, preferred_element_type=F32
    )


def nn(left, right, precision=EXACT):
    return lax.dot_general(
        left, right, (((1,), (0,)), ((), ())), precision=precision, preferred_element_type=F32
    )


def nt(left, right, precision=EXACT):
    return lax.dot_general(
        left, right, (((1,), (1,)), ((), ())), precision=precision, preferred_element_type=F32
    )


def split_tn(piece, wide):
    def thirds(value):
        first = value.astype(BF16).astype(F32)
        rest = value - first
        second = rest.astype(BF16).astype(F32)
        return first, second, rest - second

    a1, a2, a3 = thirds(piece)
    b1, b2, b3 = thirds(wide)
    left = jnp.concatenate([a1, a1, a2, a1, a2, a3], 0).astype(BF16)
    right = jnp.concatenate([b1, b2, b1, b3, b2, b1], 0).astype(BF16)
    return tn(left, right, None)


def eliminate_panel(work, first, count, panel):
    depth = 8
    start = depth * panel
    group = pl.ds(first, count)
    row_at = lax.broadcasted_iota(jnp.int32, (count, depth, 128), 1)
    rows = work[group, start : start + depth, :]
    columns = [
        jnp.broadcast_to(rows[:, :, start + j : start + j + 1], (count, depth, 128))
        for j in range(depth)
    ]
    scale = jnp.zeros((count, depth, 128), F32)
    for j in range(depth):
        column = columns[j]
        pivot = jnp.broadcast_to(column[:, j : j + 1, :], (count, depth, 128))
        scale = jnp.where(row_at == j, lax.rsqrt(pivot), scale)
        if j < depth - 1:
            share = jnp.where(row_at > j, column / pivot, 0.0)
            rows = rows - share * rows[:, j : j + 1, :]
            for k in range(j + 1, depth):
                columns[k] = columns[k] - share * columns[k][:, j : j + 1, :]
    done = rows * scale
    work[group, start : start + depth, :] = done
    after = start + depth
    if after < 64:
        for n in range(count):
            update = split_tn(done[n][:, :64], done[n])
            work[first + n, after:, :] = work[first + n, after:, :] - update[after:, :]


def kernel(
    bases_in,
    leaf_transfer_in,
    top_transfer_in,
    couplings_in,
    top_couplings_in,
    coupling_target_in,
    coupling_dest_in,
    coupling_local_in,
    top_target_in,
    top_source_in,
    leaf_bases,
    leaf_transfers,
    top_transfers,
    new_couplings,
    new_top,
    bases,
    leaf_transfer,
    top_transfer,
    couplings,
    top_couplings,
    coupling_target,
    coupling_dest,
    coupling_local,
    top_target,
    top_source,
    work,
    h_mine,
    h_theirs,
    k_mine,
    k_theirs,
    table,
    top_table,
    stacked,
    blocks,
    halves,
    in_sem,
    pair_sem,
    a_send,
    a_recv,
    ta_send,
    ta_recv,
    b_send,
    b_recv,
    s_send,
    s_recv,
):
    loads = [
        pltpu.make_async_copy(source, target, in_sem.at[n])
        for n, (source, target) in enumerate(
            [
                (bases_in, bases),
                (leaf_transfer_in, leaf_transfer),
                (top_transfer_in, top_transfer),
                (couplings_in, couplings),
                (top_couplings_in, top_couplings),
                (coupling_target_in, coupling_target),
                (coupling_dest_in, coupling_dest),
                (coupling_local_in, coupling_local),
                (top_target_in, top_target),
                (top_source_in, top_source),
            ]
        )
    ]
    for copy in loads:
        copy.start()

    me = lax.axis_index("leaf")
    near = lax.axis_index("near")
    core = me % 2
    y = (me // 2) % RING
    z = me // (2 * RING)
    a = z + core * (y - z)
    b = y + core * (z - y)

    def device(a_at, b_at):
        first = a_at + core * (b_at - a_at)
        second = b_at + core * (a_at - b_at)
        return {"leaf": (first * RING + second) * 2 + core}

    def wrap(value):
        return (value + 2 * RING) % RING

    b_right, b_left = device(a, wrap(b + 1)), device(a, wrap(b - 1))
    sibling = {"leaf": me + 1 - 2 * core}
    cousin = {"leaf": me + 2 - 4 * ((me // 2) % 2)}
    parity = core
    upper = (me // 2) % 2

    barrier = pltpu.get_barrier_semaphore()
    partners = [sibling, b_right, b_left] + [device(wrap(a + k), b) for k in range(1, RING)]
    for partner in partners:
        pl.semaphore_signal(barrier, inc=1, device_id=partner, device_id_type=MESH)

    def remote(source, target, send, recv, to):
        return pltpu.make_async_remote_copy(
            src_ref=source,
            dst_ref=target,
            send_sem=send,
            recv_sem=recv,
            device_id=to,
            device_id_type=MESH,
        )

    def row_of(b_at, a_at):
        return core * 64 + b_at * RING + a_at

    started = []

    def go(copy):
        copy.start()
        started.append(copy)

    row = lax.broadcasted_iota(jnp.int32, (64, 128), 0)
    lane = lax.broadcasted_iota(jnp.int32, (64, 128), 1)
    keep = row <= lane % 64
    low_lane = lane < 64
    unit = jnp.where(row == lane - 64, 1.0, 0.0)
    row32 = lax.broadcasted_iota(jnp.int32, (32, 128), 0)
    lane32 = lax.broadcasted_iota(jnp.int32, (32, 128), 1)

    for n in range(20):
        work[n] = unit
    loads[0].wait()
    loads[1].wait()
    for n in range(8):
        gram = tn(bases[n], bases[n])
        work[n, :, 0:64] = gram
        h_mine[n] = tn(leaf_transfer[n], nn(gram, leaf_transfer[n]))
    pl.semaphore_wait(barrier, len(partners))
    to_sibling = remote(h_mine, h_theirs, pair_sem.at[0], pair_sem.at[1], sibling)
    to_sibling.start()

    for panel in range(4):
        eliminate_panel(work, 0, 8, panel)

    to_sibling.wait()
    loads[2].wait()
    for n in range(8):
        work[8 + n, :, 0:64] = h_mine[n] + h_theirs[n]
    for n in range(4):
        mid = work[8 + parity * 4 + n][:, 0:64]
        k_mine[n] = tn(top_transfer[n], nn(mid, top_transfer[n]))
    to_cousin = remote(k_mine, k_theirs, pair_sem.at[2], pair_sem.at[3], cousin)
    to_cousin.start()

    for panel in range(4, 8):
        eliminate_panel(work, 0, 8, panel)

    def pair_of(first, second):
        both = jnp.where(low_lane, first, pltpu.roll(second, 64, 1))
        return jnp.where(keep, both, 0.0).astype(BF16)

    for g in range(2):
        f0, f1, f2, f3 = (work[4 * g + i] for i in range(4))
        tile = row_of(b, a) * 6 + 3 * g
        table[tile] = pair_of(f0, f1)[0:32]
        table[tile + 1] = pair_of(f2, f3)[0:32]
        corner = jnp.where(
            lane32 < 64,
            jnp.where(lane32 < 32, pltpu.roll(f0[32:64], 96, 1), f1[32:64]),
            jnp.where(lane32 < 96, pltpu.roll(f2[32:64], 32, 1), pltpu.roll(f3[32:64], 64, 1)),
        )
        table[tile + 2] = jnp.where(row32 <= lane32 % 32, corner, 0.0).astype(BF16)

    def own_sends(span, send, recv):
        for k in (4, 3, 5, 2, 6, 1, 7):
            go(remote(span, span, send.at[k], recv.at[k], device(wrap(a + k), b)))

    offsets = [0, 1, -1, 2, -2, 3, -3, 4]

    def own_arrival(w, span_of, send, recv):
        if w > 0:
            k = offsets[w] % RING
            span = span_of(wrap(a - k))
            remote(span, span, send.at[k], recv.at[k], sibling).wait_recv()

    def leaf_item(a_at):
        return table.at[pl.ds(row_of(b, a_at) * 6, 6)]

    def top_item(a_at):
        return top_table.at[row_of(b, a_at)]

    def span_at(b_at, piece, part=None):
        if piece < 8:
            return table.at[pl.ds(row_of(b_at, wrap(a - offsets[piece])) * 6, 6)]
        low, size = (0, 8) if part is None else (4 * part, 4)
        return top_table.at[pl.ds(row_of(b_at, 0) + low, size)]

    def hop(h, piece, way):
        if h == 4 and piece < 8 and (piece % 2 == 0) != (way > 0):
            return None
        return h, piece, (way < 0) * 1 if h == 4 else None

    def b_slot(h, piece, way):
        return ((h - 1) * 2 + (way > 0)) * 9 + piece

    def forward(h, piece):
        for way in (1, -1):
            kind = hop(h + 1, piece, way)
            if kind is not None:
                span = span_at(wrap(b - way * h), piece, kind[2])
                slot = b_slot(h + 1, piece, way)
                to = b_right if way > 0 else b_left
                go(remote(span, span, b_send.at[slot], b_recv.at[slot], to))

    def arrive(h, piece):
        for way in (1, -1):
            kind = hop(h, piece, way)
            if kind is not None:
                span = span_at(wrap(b - way * h), piece, kind[2])
                slot = b_slot(h, piece, way)
                remote(span, span, b_send.at[slot], b_recv.at[slot], sibling).wait_recv()

    b_offsets = [0, -1, 1, -2, 2, -3, 3, 4]

    def row_span(place, part):
        if part < 2:
            return table.at[pl.ds((place + 4 * part) * 6, 24)]
        return top_table.at[pl.ds(place, 8)]

    def hand_over(h, part):
        for slot, offset in enumerate(b_offsets):
            if abs(offset) == h:
                span = row_span(row_of(wrap(b + offset), 0), part)
                at = slot * 3 + part
                go(remote(span, span, s_send.at[at], s_recv.at[at], sibling))

    def handed(part):
        for slot, offset in enumerate(b_offsets):
            span = row_span((1 - core) * 64 + wrap(a + offset) * RING, part)
            at = slot * 3 + part
            remote(span, span, s_send.at[at], s_recv.at[at], sibling).wait_recv()

    def second_ring(h, piece):
        if h > 0:
            arrive(h, piece)
        elif piece < 8:
            own_arrival(piece, leaf_item, a_send, a_recv)
        else:
            for w in range(8):
                own_arrival(w, top_item, ta_send, ta_recv)
        if h < 4:
            forward(h, piece)
        if piece == 7:
            hand_over(h, 0)
            hand_over(h, 1)
        elif piece == 8:
            hand_over(h, 2)

    def factor(n):
        return jnp.where(keep, work[n], 0.0)[:, 0:64]

    def inverse_transposed(n):
        return work[n][:, 64:128]

    def finish_bases():
        for k in range(2):
            at = near * 2 + k
            leaf_bases[k] = nt(bases[at], inverse_transposed(at))

    def finish_leaf(n):
        piece = nn(factor(n), leaf_transfer[n])
        leaf_transfers[n] = nt(piece, inverse_transposed(8 + n))

    def finish_top(n):
        piece = nn(factor(8 + parity * 4 + n), top_transfer[n])
        top_transfers[n] = nt(piece, inverse_transposed(16 + n))

    def stack_factors():
        for n in range(8):
            low = factor(n).astype(BF16)
            stacked[n] = jnp.concatenate([low[:, :32], low[:, 32:]], 0)

    def unpack_blocks(first, last):
        for k in range(first, last):
            slab = jnp.concatenate([couplings[k].astype(F32), couplings[k + 32].astype(F32)], 0)
            blocks[pl.ds(k, 128, stride=32), :] = jnp.transpose(slab)

    def half_step(first, last):
        for n in range(first, last):
            block = blocks[32 * n : 32 * n + 32, :].astype(BF16)
            both = nn(stacked[coupling_target[n]], block, None)
            mixed = jnp.where(low_lane, both[0:64], both[64:128])
            mixed = mixed + pltpu.roll(mixed, 64, 1)
            right = jnp.where((lane // 32) % 2 == 1, mixed, pltpu.roll(mixed, 32, 1))
            local = coupling_local[n] & 3
            mixed = jnp.where(lane // 64 == (local & 1), mixed, 0.0)
            right = jnp.where(lane // 32 == local, right, 0.0)
            halves[n, :, 0:128] = mixed.astype(BF16)
            halves[n, :, 128:256] = right.astype(BF16)

    own_sends(leaf_item(a), a_send, a_recv)

    to_cousin.wait()
    for n in range(4):
        work[16 + n, :, 0:64] = k_mine[n] + k_theirs[n]
    for panel in range(8):
        eliminate_panel(work, 8, 12, panel)
        if panel == 3:
            for piece in range(5):
                second_ring(0, piece)
        if panel == 5:
            for piece in range(5, 8):
                second_ring(0, piece)

    top_table[row_of(b, a)] = pair_of(work[16 + upper * 2], work[17 + upper * 2])
    own_sends(top_item(a), ta_send, ta_recv)

    for copy in loads[3:]:
        copy.wait()
    stack_factors()

    queue = [functools.partial(unpack_blocks, k, k + 4) for k in range(0, 32, 4)]
    queue += [functools.partial(half_step, n, n + 8) for n in range(0, 128, 8)]
    queue += [finish_bases]
    queue += [functools.partial(finish_leaf, n) for n in range(8)]
    queue += [functools.partial(finish_top, n) for n in range(4)]

    events = [(1, w) for w in range(8)] + [(0, 8)]
    events += [(2, w) for w in range(4)] + [(1, 8)] + [(2, w) for w in range(4, 8)]
    events += [(3, w) for w in range(4)] + [(2, 8)] + [(3, w) for w in range(4, 8)]
    events += [(3, 8)] + [(4, w) for w in range(8)] + [(4, 8)]
    for h, piece in events:
        second_ring(h, piece)
        if queue:
            queue.pop(0)()
    while queue:
        queue.pop(0)()

    handed(0)
    handed(1)

    def table_row(leaf_place):
        c = leaf_place & 1
        y_at = (leaf_place >> 1) & 7
        z_at = leaf_place >> 4
        return c * 64 + (y_at + c * (z_at - y_at)) * RING + z_at + c * (y_at - z_at)

    empty = jnp.zeros((32, 128), BF16)
    for n in range(128):
        local = coupling_local[n]
        tile = table_row(coupling_dest[n]) * 6 + (local >> 2) * 3
        upper_rows = jnp.concatenate([table[tile + ((local >> 1) & 1)], empty], 1)
        lower_rows = jnp.concatenate([empty, table[tile + 2]], 1)
        new = nt(halves[n], jnp.concatenate([upper_rows, lower_rows], 0), None)
        blocks[32 * n : 32 * n + 32, :] = jnp.concatenate([new[0:32], new[32:64]], 1)
    for k in range(32):
        slab = jnp.transpose(blocks[pl.ds(k, 128, stride=32), :]).astype(BF16)
        new_couplings[k] = slab[0:64]
        new_couplings[k + 32] = slab[64:128]

    handed(2)
    quad = me // 4

    def top_tile(cluster):
        place = (cluster >> 3) * 4 + (cluster & 2) + ((cluster >> 2) & 1)
        return top_table[table_row(place)]

    for n in range(16):
        target = quad * 8 + top_target[n]
        source = top_source[n]
        left = jnp.where((lane // 64) == (target & 1), top_tile(target), jnp.zeros((), BF16))
        block = top_couplings[n]
        double = jnp.concatenate([block, block], 1)
        half = nn(left, jnp.concatenate([double, double], 0), None)
        half = jnp.where((lane // 64) == (source & 1), half, 0.0).astype(BF16)
        new_top[n] = nt(half, top_tile(source), None).astype(BF16)

    for copy in started:
        copy.wait_send()


def hand_out(*refs):
    count = len(refs) // 2
    sems = refs[-1]
    copies = [
        pltpu.make_async_copy(refs[n], refs[count + n], sems.at[n]) for n in range(count)
    ]
    for copy in copies:
        copy.start()
    for copy in copies:
        copy.wait()


def on_device(
    bases,
    leaf_transfer,
    top_transfer,
    couplings,
    coupling_target,
    coupling_dest,
    coupling_local,
    top_couplings,
    top_target,
    top_source,
):
    vmem = pl.BlockSpec(memory_space=pltpu.VMEM)
    anywhere = pl.BlockSpec(memory_space=pl.ANY)
    dma = pltpu.SemaphoreType.DMA
    shapes = (
        jax.ShapeDtypeStruct((2, 64, 64), F32),
        jax.ShapeDtypeStruct((8, 64, 64), F32),
        jax.ShapeDtypeStruct((4, 64, 64), F32),
        jax.ShapeDtypeStruct((64, 64, 128), BF16),
        jax.ShapeDtypeStruct((16, 64, 64), BF16),
    )
    results = pl.pallas_call(
        kernel,
        out_shape=shapes,
        in_specs=[anywhere] * 10,
        out_specs=[vmem] * 5,
        scratch_shapes=[
            pltpu.VMEM((8, 64, 64), F32),
            pltpu.VMEM((8, 64, 64), F32),
            pltpu.VMEM((4, 64, 64), F32),
            pltpu.VMEM((64, 64, 128), BF16),
            pltpu.VMEM((16, 64, 64), BF16),
            pltpu.SMEM((128,), jnp.int32),
            pltpu.SMEM((128,), jnp.int32),
            pltpu.SMEM((128,), jnp.int32),
            pltpu.SMEM((16,), jnp.int32),
            pltpu.SMEM((16,), jnp.int32),
            pltpu.VMEM((20, 64, 128), F32),
            pltpu.VMEM((8, 64, 64), F32),
            pltpu.VMEM((8, 64, 64), F32),
            pltpu.VMEM((4, 64, 64), F32),
            pltpu.VMEM((4, 64, 64), F32),
            pltpu.VMEM((768, 32, 128), BF16),
            pltpu.VMEM((128, 64, 128), BF16),
            pltpu.VMEM((8, 128, 32), BF16),
            pltpu.VMEM((4096, 128), F32),
            pltpu.VMEM((128, 64, 256), BF16),
            dma((10,)),
            dma((4,)),
            dma((8,)),
            dma((8,)),
            dma((8,)),
            dma((8,)),
            dma((72,)),
            dma((72,)),
            dma((24,)),
            dma((24,)),
        ],
        compiler_params=pltpu.CompilerParams(
            collective_id=0, has_side_effects=True, vmem_limit_bytes=58 * 2**20
        ),
    )(
        bases,
        leaf_transfer,
        top_transfer,
        jnp.transpose(couplings, (1, 2, 0)),
        top_couplings,
        coupling_target,
        coupling_dest[:, 0],
        coupling_local,
        top_target,
        top_source,
    )
    leaf_bases, leaf_transfers, top_transfers, new_couplings, new_top = pl.pallas_call(
        hand_out,
        out_shape=shapes,
        in_specs=[vmem] * 5,
        out_specs=[anywhere] * 5,
        scratch_shapes=[dma((5,))],
    )(*results)
    return (
        leaf_bases,
        leaf_transfers,
        top_transfers,
        jnp.transpose(new_couplings, (2, 0, 1)),
        new_top,
    )


def solution(mesh):
    in_specs = (
        P("leaf", None, None),
        P("leaf", None, None),
        P("leaf", None, None),
        P(("leaf", "near"), None, None),
        P(("leaf", "near")),
        P(("leaf", "near"), None),
        P(("leaf", "near")),
        P(("leaf", "near"), None, None),
        P(("leaf", "near")),
        P(("leaf", "near")),
    )
    out_specs = (
        P(("leaf", "near"), None, None),
        P("leaf", None, None),
        P("leaf", None, None),
        P(("leaf", "near"), None, None),
        P(("leaf", "near"), None, None),
    )
    return jax.shard_map(
        on_device, mesh=mesh, in_specs=in_specs, out_specs=out_specs, check_vma=False
    )
```

```python
import functools

import jax
import jax.numpy as jnp
from jax import lax
from jax.experimental import pallas as pl
from jax.experimental.pallas import tpu as pltpu
from jax.sharding import PartitionSpec as P

MESH = pl.DeviceIdType.MESH
F32 = jnp.float32
BF16 = jnp.bfloat16
EXACT = lax.Precision.HIGHEST
RING = 8


def tn(left, right, precision=EXACT):
    return lax.dot_general(
        left, right, (((0,), (0,)), ((), ())), precision=precision, preferred_element_type=F32
    )


def nn(left, right, precision=EXACT):
    return lax.dot_general(
        left, right, (((1,), (0,)), ((), ())), precision=precision, preferred_element_type=F32
    )


def nt(left, right, precision=EXACT):
    return lax.dot_general(
        left, right, (((1,), (1,)), ((), ())), precision=precision, preferred_element_type=F32
    )


def split_tn(piece, wide):
    def thirds(value):
        first = value.astype(BF16).astype(F32)
        rest = value - first
        second = rest.astype(BF16).astype(F32)
        return first, second, rest - second

    a1, a2, a3 = thirds(piece)
    b1, b2, b3 = thirds(wide)
    left = jnp.concatenate([a1, a1, a2, a1, a2, a3], 0).astype(BF16)
    right = jnp.concatenate([b1, b2, b1, b3, b2, b1], 0).astype(BF16)
    return tn(left, right, None)


def eliminate_panel(work, first, count, panel):
    depth = 8
    start = depth * panel
    group = pl.ds(first, count)
    row_at = lax.broadcasted_iota(jnp.int32, (count, depth, 128), 1)
    rows = work[group, start : start + depth, :]
    columns = [
        jnp.broadcast_to(rows[:, :, start + j : start + j + 1], (count, depth, 128))
        for j in range(depth)
    ]
    scale = jnp.zeros((count, depth, 128), F32)
    for j in range(depth):
        column = columns[j]
        pivot = jnp.broadcast_to(column[:, j : j + 1, :], (count, depth, 128))
        scale = jnp.where(row_at == j, lax.rsqrt(pivot), scale)
        if j < depth - 1:
            share = jnp.where(row_at > j, column / pivot, 0.0)
            rows = rows - share * rows[:, j : j + 1, :]
            for k in range(j + 1, depth):
                columns[k] = columns[k] - share * columns[k][:, j : j + 1, :]
    done = rows * scale
    work[group, start : start + depth, :] = done
    after = start + depth
    if after < 64:
        for n in range(count):
            update = split_tn(done[n][:, :64], done[n])
            work[first + n, after:, :] = work[first + n, after:, :] - update[after:, :]


def kernel(
    bases_in,
    leaf_transfer_in,
    top_transfer_in,
    couplings_in,
    top_couplings_in,
    coupling_target_in,
    coupling_dest_in,
    coupling_local_in,
    top_target_in,
    top_source_in,
    leaf_bases,
    leaf_transfers,
    top_transfers,
    new_couplings,
    new_top,
    bases,
    leaf_transfer,
    top_transfer,
    couplings,
    top_couplings,
    coupling_target,
    coupling_dest,
    coupling_local,
    top_target,
    top_source,
    work,
    h_mine,
    h_theirs,
    k_mine,
    k_theirs,
    table,
    top_table,
    stacked,
    blocks,
    halves,
    in_sem,
    pair_sem,
    a_send,
    a_recv,
    ta_send,
    ta_recv,
    b_send,
    b_recv,
    s_send,
    s_recv,
):
    loads = [
        pltpu.make_async_copy(source, target, in_sem.at[n])
        for n, (source, target) in enumerate(
            [
                (bases_in, bases),
                (leaf_transfer_in, leaf_transfer),
                (top_transfer_in, top_transfer),
                (couplings_in, couplings),
                (top_couplings_in, top_couplings),
                (coupling_target_in, coupling_target),
                (coupling_dest_in, coupling_dest),
                (coupling_local_in, coupling_local),
                (top_target_in, top_target),
                (top_source_in, top_source),
            ]
        )
    ]
    for copy in loads:
        copy.start()

    me = lax.axis_index("leaf")
    near = lax.axis_index("near")
    core = me % 2
    y = (me // 2) % RING
    z = me // (2 * RING)
    a = z + core * (y - z)
    b = y + core * (z - y)

    def device(a_at, b_at):
        first = a_at + core * (b_at - a_at)
        second = b_at + core * (a_at - b_at)
        return {"leaf": (first * RING + second) * 2 + core}

    def wrap(value):
        return (value + 2 * RING) % RING

    b_right, b_left = device(a, wrap(b + 1)), device(a, wrap(b - 1))
    sibling = {"leaf": me + 1 - 2 * core}
    cousin = {"leaf": me + 2 - 4 * ((me // 2) % 2)}
    parity = core
    upper = (me // 2) % 2

    barrier = pltpu.get_barrier_semaphore()
    partners = [sibling, b_right, b_left] + [device(wrap(a + k), b) for k in range(1, RING)]
    for partner in partners:
        pl.semaphore_signal(barrier, inc=1, device_id=partner, device_id_type=MESH)

    def remote(source, target, send, recv, to):
        return pltpu.make_async_remote_copy(
            src_ref=source,
            dst_ref=target,
            send_sem=send,
            recv_sem=recv,
            device_id=to,
            device_id_type=MESH,
        )

    def row_of(b_at, a_at):
        return core * 64 + b_at * RING + a_at

    started = []

    def go(copy):
        copy.start()
        started.append(copy)

    row = lax.broadcasted_iota(jnp.int32, (64, 128), 0)
    lane = lax.broadcasted_iota(jnp.int32, (64, 128), 1)
    keep = row <= lane % 64
    low_lane = lane < 64
    unit = jnp.where(row == lane - 64, 1.0, 0.0)
    row32 = lax.broadcasted_iota(jnp.int32, (32, 128), 0)
    lane32 = lax.broadcasted_iota(jnp.int32, (32, 128), 1)

    for n in range(20):
        work[n] = unit
    loads[0].wait()
    loads[1].wait()
    for n in range(8):
        gram = tn(bases[n], bases[n])
        work[n, :, 0:64] = gram
        h_mine[n] = tn(leaf_transfer[n], nn(gram, leaf_transfer[n]))
    pl.semaphore_wait(barrier, len(partners))
    to_sibling = remote(h_mine, h_theirs, pair_sem.at[0], pair_sem.at[1], sibling)
    to_sibling.start()

    for panel in range(4):
        eliminate_panel(work, 0, 8, panel)

    to_sibling.wait()
    loads[2].wait()
    for n in range(8):
        work[8 + n, :, 0:64] = h_mine[n] + h_theirs[n]
    for n in range(4):
        mid = work[8 + parity * 4 + n][:, 0:64]
        k_mine[n] = tn(top_transfer[n], nn(mid, top_transfer[n]))
    to_cousin = remote(k_mine, k_theirs, pair_sem.at[2], pair_sem.at[3], cousin)
    to_cousin.start()

    for panel in range(4, 8):
        eliminate_panel(work, 0, 8, panel)

    def pair_of(first, second):
        both = jnp.where(low_lane, first, pltpu.roll(second, 64, 1))
        return jnp.where(keep, both, 0.0).astype(BF16)

    for g in range(2):
        f0, f1, f2, f3 = (work[4 * g + i] for i in range(4))
        tile = row_of(b, a) * 6 + 3 * g
        table[tile] = pair_of(f0, f1)[0:32]
        table[tile + 1] = pair_of(f2, f3)[0:32]
        corner = jnp.where(
            lane32 < 64,
            jnp.where(lane32 < 32, pltpu.roll(f0[32:64], 96, 1), f1[32:64]),
            jnp.where(lane32 < 96, pltpu.roll(f2[32:64], 32, 1), pltpu.roll(f3[32:64], 64, 1)),
        )
        table[tile + 2] = jnp.where(row32 <= lane32 % 32, corner, 0.0).astype(BF16)

    def own_sends(span, send, recv):
        for k in (1, 7, 2, 6, 3, 5, 4):
            go(remote(span, span, send.at[k], recv.at[k], device(wrap(a + k), b)))

    offsets = [0, 1, -1, 2, -2, 3, -3, 4]

    def own_arrival(w, span_of, send, recv):
        if w > 0:
            k = offsets[w] % RING
            span = span_of(wrap(a - k))
            remote(span, span, send.at[k], recv.at[k], sibling).wait_recv()

    def leaf_item(a_at):
        return table.at[pl.ds(row_of(b, a_at) * 6, 6)]

    def top_item(a_at):
        return top_table.at[row_of(b, a_at)]

    def span_at(b_at, piece, part=None):
        if piece < 8:
            return table.at[pl.ds(row_of(b_at, wrap(a - offsets[piece])) * 6, 6)]
        low, size = (0, 8) if part is None else (4 * part, 4)
        return top_table.at[pl.ds(row_of(b_at, 0) + low, size)]

    def hop(h, piece, way):
        if h == 4 and piece < 8 and (piece % 2 == 0) != (way > 0):
            return None
        return h, piece, (way < 0) * 1 if h == 4 else None

    def b_slot(h, piece, way):
        return ((h - 1) * 2 + (way > 0)) * 9 + piece

    def forward(h, piece):
        for way in (1, -1):
            kind = hop(h + 1, piece, way)
            if kind is not None:
                span = span_at(wrap(b - way * h), piece, kind[2])
                slot = b_slot(h + 1, piece, way)
                to = b_right if way > 0 else b_left
                go(remote(span, span, b_send.at[slot], b_recv.at[slot], to))

    def arrive(h, piece):
        for way in (1, -1):
            kind = hop(h, piece, way)
            if kind is not None:
                span = span_at(wrap(b - way * h), piece, kind[2])
                slot = b_slot(h, piece, way)
                remote(span, span, b_send.at[slot], b_recv.at[slot], sibling).wait_recv()

    b_offsets = [0, -1, 1, -2, 2, -3, 3, 4]

    def row_span(place, part):
        if part < 2:
            return table.at[pl.ds((place + 4 * part) * 6, 24)]
        return top_table.at[pl.ds(place, 8)]

    def hand_over(h, part):
        for slot, offset in enumerate(b_offsets):
            if abs(offset) == h:
                span = row_span(row_of(wrap(b + offset), 0), part)
                at = slot * 3 + part
                go(remote(span, span, s_send.at[at], s_recv.at[at], sibling))

    def handed(part):
        for slot, offset in enumerate(b_offsets):
            span = row_span((1 - core) * 64 + wrap(a + offset) * RING, part)
            at = slot * 3 + part
            remote(span, span, s_send.at[at], s_recv.at[at], sibling).wait_recv()

    def second_ring(h, piece):
        if h > 0:
            arrive(h, piece)
        elif piece < 8:
            own_arrival(piece, leaf_item, a_send, a_recv)
        else:
            for w in range(8):
                own_arrival(w, top_item, ta_send, ta_recv)
        if h < 4:
            forward(h, piece)
        if piece == 7:
            hand_over(h, 0)
            hand_over(h, 1)
        elif piece == 8:
            hand_over(h, 2)

    def factor(n):
        return jnp.where(keep, work[n], 0.0)[:, 0:64]

    def inverse_transposed(n):
        return work[n][:, 64:128]

    def finish_bases():
        for k in range(2):
            at = near * 2 + k
            leaf_bases[k] = nt(bases[at], inverse_transposed(at))

    def finish_leaf(n):
        piece = nn(factor(n), leaf_transfer[n])
        leaf_transfers[n] = nt(piece, inverse_transposed(8 + n))

    def finish_top(n):
        piece = nn(factor(8 + parity * 4 + n), top_transfer[n])
        top_transfers[n] = nt(piece, inverse_transposed(16 + n))

    def stack_factors():
        for n in range(8):
            low = factor(n).astype(BF16)
            stacked[n] = jnp.concatenate([low[:, :32], low[:, 32:]], 0)

    def unpack_blocks(first, last):
        for k in range(first, last):
            slab = jnp.concatenate([couplings[k].astype(F32), couplings[k + 32].astype(F32)], 0)
            blocks[pl.ds(k, 128, stride=32), :] = jnp.transpose(slab)

    def half_step(first, last):
        for n in range(first, last):
            block = blocks[32 * n : 32 * n + 32, :].astype(BF16)
            both = nn(stacked[coupling_target[n]], block, None)
            mixed = jnp.where(low_lane, both[0:64], both[64:128])
            mixed = mixed + pltpu.roll(mixed, 64, 1)
            right = jnp.where((lane // 32) % 2 == 1, mixed, pltpu.roll(mixed, 32, 1))
            local = coupling_local[n] & 3
            mixed = jnp.where(lane // 64 == (local & 1), mixed, 0.0)
            right = jnp.where(lane // 32 == local, right, 0.0)
            halves[n, :, 0:128] = mixed.astype(BF16)
            halves[n, :, 128:256] = right.astype(BF16)

    own_sends(leaf_item(a), a_send, a_recv)
    second_ring(0, 0)

    to_cousin.wait()
    for n in range(4):
        work[16 + n, :, 0:64] = k_mine[n] + k_theirs[n]
    for panel in range(8):
        eliminate_panel(work, 16, 4, panel)

    top_table[row_of(b, a)] = pair_of(work[16 + upper * 2], work[17 + upper * 2])
    own_sends(top_item(a), ta_send, ta_recv)

    for copy in loads[3:]:
        copy.wait()
    stack_factors()

    queue = [functools.partial(unpack_blocks, k, k + 4) for k in range(0, 32, 4)]
    queue += [functools.partial(half_step, n, n + 8) for n in range(0, 128, 8)]
    queue += [functools.partial(eliminate_panel, work, 8, 8, panel) for panel in range(8)]
    queue += [finish_bases]
    queue += [functools.partial(finish_leaf, n) for n in range(8)]
    queue += [functools.partial(finish_top, n) for n in range(4)]

    leaf_events = [(h, w) for h in range(5) for w in range(8)][1:]
    events = []
    for h, w in sorted(leaf_events, key=lambda at: (at[1] + 6 * at[0], -at[0])):
        events.append((h, w))
        if w == 7:
            events.append((h, 8))
    for h, piece in events:
        second_ring(h, piece)
        if queue:
            queue.pop(0)()
    while queue:
        queue.pop(0)()

    handed(0)
    handed(1)

    def table_row(leaf_place):
        c = leaf_place & 1
        y_at = (leaf_place >> 1) & 7
        z_at = leaf_place >> 4
        return c * 64 + (y_at + c * (z_at - y_at)) * RING + z_at + c * (y_at - z_at)

    empty = jnp.zeros((32, 128), BF16)
    for n in range(128):
        local = coupling_local[n]
        tile = table_row(coupling_dest[n]) * 6 + (local >> 2) * 3
        upper_rows = jnp.concatenate([table[tile + ((local >> 1) & 1)], empty], 1)
        lower_rows = jnp.concatenate([empty, table[tile + 2]], 1)
        new = nt(halves[n], jnp.concatenate([upper_rows, lower_rows], 0), None)
        blocks[32 * n : 32 * n + 32, :] = jnp.concatenate([new[0:32], new[32:64]], 1)
    for k in range(32):
        slab = jnp.transpose(blocks[pl.ds(k, 128, stride=32), :]).astype(BF16)
        new_couplings[k] = slab[0:64]
        new_couplings[k + 32] = slab[64:128]

    handed(2)
    quad = me // 4

    def top_tile(cluster):
        place = (cluster >> 3) * 4 + (cluster & 2) + ((cluster >> 2) & 1)
        return top_table[table_row(place)]

    for n in range(16):
        target = quad * 8 + top_target[n]
        source = top_source[n]
        left = jnp.where((lane // 64) == (target & 1), top_tile(target), jnp.zeros((), BF16))
        block = top_couplings[n]
        double = jnp.concatenate([block, block], 1)
        half = nn(left, jnp.concatenate([double, double], 0), None)
        half = jnp.where((lane // 64) == (source & 1), half, 0.0).astype(BF16)
        new_top[n] = nt(half, top_tile(source), None).astype(BF16)

    for copy in started:
        copy.wait_send()


def hand_out(*refs):
    count = len(refs) // 2
    sems = refs[-1]
    copies = [
        pltpu.make_async_copy(refs[n], refs[count + n], sems.at[n]) for n in range(count)
    ]
    for copy in copies:
        copy.start()
    for copy in copies:
        copy.wait()


def on_device(
    bases,
    leaf_transfer,
    top_transfer,
    couplings,
    coupling_target,
    coupling_dest,
    coupling_local,
    top_couplings,
    top_target,
    top_source,
):
    vmem = pl.BlockSpec(memory_space=pltpu.VMEM)
    anywhere = pl.BlockSpec(memory_space=pl.ANY)
    dma = pltpu.SemaphoreType.DMA
    shapes = (
        jax.ShapeDtypeStruct((2, 64, 64), F32),
        jax.ShapeDtypeStruct((8, 64, 64), F32),
        jax.ShapeDtypeStruct((4, 64, 64), F32),
        jax.ShapeDtypeStruct((64, 64, 128), BF16),
        jax.ShapeDtypeStruct((16, 64, 64), BF16),
    )
    results = pl.pallas_call(
        kernel,
        out_shape=shapes,
        in_specs=[anywhere] * 10,
        out_specs=[vmem] * 5,
        scratch_shapes=[
            pltpu.VMEM((8, 64, 64), F32),
            pltpu.VMEM((8, 64, 64), F32),
            pltpu.VMEM((4, 64, 64), F32),
            pltpu.VMEM((64, 64, 128), BF16),
            pltpu.VMEM((16, 64, 64), BF16),
            pltpu.SMEM((128,), jnp.int32),
            pltpu.SMEM((128,), jnp.int32),
            pltpu.SMEM((128,), jnp.int32),
            pltpu.SMEM((16,), jnp.int32),
            pltpu.SMEM((16,), jnp.int32),
            pltpu.VMEM((20, 64, 128), F32),
            pltpu.VMEM((8, 64, 64), F32),
            pltpu.VMEM((8, 64, 64), F32),
            pltpu.VMEM((4, 64, 64), F32),
            pltpu.VMEM((4, 64, 64), F32),
            pltpu.VMEM((768, 32, 128), BF16),
            pltpu.VMEM((128, 64, 128), BF16),
            pltpu.VMEM((8, 128, 32), BF16),
            pltpu.VMEM((4096, 128), F32),
            pltpu.VMEM((128, 64, 256), BF16),
            dma((10,)),
            dma((4,)),
            dma((8,)),
            dma((8,)),
            dma((8,)),
            dma((8,)),
            dma((72,)),
            dma((72,)),
            dma((24,)),
            dma((24,)),
        ],
        compiler_params=pltpu.CompilerParams(
            collective_id=0, has_side_effects=True, vmem_limit_bytes=58 * 2**20
        ),
    )(
        bases,
        leaf_transfer,
        top_transfer,
        jnp.transpose(couplings, (1, 2, 0)),
        top_couplings,
        coupling_target,
        coupling_dest[:, 0],
        coupling_local,
        top_target,
        top_source,
    )
    leaf_bases, leaf_transfers, top_transfers, new_couplings, new_top = pl.pallas_call(
        hand_out,
        out_shape=shapes,
        in_specs=[vmem] * 5,
        out_specs=[anywhere] * 5,
        scratch_shapes=[dma((5,))],
    )(*results)
    return (
        leaf_bases,
        leaf_transfers,
        top_transfers,
        jnp.transpose(new_couplings, (2, 0, 1)),
        new_top,
    )


def solution(mesh):
    in_specs = (
        P("leaf", None, None),
        P("leaf", None, None),
        P("leaf", None, None),
        P(("leaf", "near"), None, None),
        P(("leaf", "near")),
        P(("leaf", "near"), None),
        P(("leaf", "near")),
        P(("leaf", "near"), None, None),
        P(("leaf", "near")),
        P(("leaf", "near")),
    )
    out_specs = (
        P(("leaf", "near"), None, None),
        P("leaf", None, None),
        P("leaf", None, None),
        P(("leaf", "near"), None, None),
        P(("leaf", "near"), None, None),
    )
    return jax.shard_map(
        on_device, mesh=mesh, in_specs=in_specs, out_specs=out_specs, check_vma=False
    )
```

```python
import functools

import jax
import jax.numpy as jnp
from jax import lax
from jax.experimental import pallas as pl
from jax.experimental.pallas import tpu as pltpu
from jax.sharding import PartitionSpec as P

MESH = pl.DeviceIdType.MESH
F32 = jnp.float32
BF16 = jnp.bfloat16
EXACT = lax.Precision.HIGHEST
RING = 8


def tn(left, right, precision=EXACT):
    return lax.dot_general(
        left, right, (((0,), (0,)), ((), ())), precision=precision, preferred_element_type=F32
    )


def nn(left, right, precision=EXACT):
    return lax.dot_general(
        left, right, (((1,), (0,)), ((), ())), precision=precision, preferred_element_type=F32
    )


def nt(left, right, precision=EXACT):
    return lax.dot_general(
        left, right, (((1,), (1,)), ((), ())), precision=precision, preferred_element_type=F32
    )


def split_tn(piece, wide):
    def thirds(value):
        first = value.astype(BF16).astype(F32)
        rest = value - first
        second = rest.astype(BF16).astype(F32)
        return first, second, rest - second

    a1, a2, a3 = thirds(piece)
    b1, b2, b3 = thirds(wide)
    left = jnp.concatenate([a1, a1, a2, a1, a2, a3], 0).astype(BF16)
    right = jnp.concatenate([b1, b2, b1, b3, b2, b1], 0).astype(BF16)
    return tn(left, right, None)


def eliminate_panel(work, first, count, panel):
    depth = 8
    start = depth * panel
    group = pl.ds(first, count)
    row_at = lax.broadcasted_iota(jnp.int32, (count, depth, 128), 1)
    rows = work[group, start : start + depth, :]
    columns = [
        jnp.broadcast_to(rows[:, :, start + j : start + j + 1], (count, depth, 128))
        for j in range(depth)
    ]
    scale = jnp.zeros((count, depth, 128), F32)
    for j in range(depth):
        column = columns[j]
        pivot = jnp.broadcast_to(column[:, j : j + 1, :], (count, depth, 128))
        scale = jnp.where(row_at == j, lax.rsqrt(pivot), scale)
        if j < depth - 1:
            share = jnp.where(row_at > j, column / pivot, 0.0)
            rows = rows - share * rows[:, j : j + 1, :]
            for k in range(j + 1, depth):
                columns[k] = columns[k] - share * columns[k][:, j : j + 1, :]
    done = rows * scale
    work[group, start : start + depth, :] = done
    after = start + depth
    if after < 64:
        for n in range(count):
            update = split_tn(done[n][:, :64], done[n])
            work[first + n, after:, :] = work[first + n, after:, :] - update[after:, :]


def kernel(
    bases_in,
    leaf_transfer_in,
    top_transfer_in,
    couplings_in,
    top_couplings_in,
    coupling_target_in,
    coupling_dest_in,
    coupling_local_in,
    top_target_in,
    top_source_in,
    leaf_bases,
    leaf_transfers,
    top_transfers,
    new_couplings,
    new_top,
    bases,
    leaf_transfer,
    top_transfer,
    couplings,
    top_couplings,
    coupling_target,
    coupling_dest,
    coupling_local,
    top_target,
    top_source,
    work,
    h_mine,
    h_theirs,
    k_mine,
    k_theirs,
    table,
    top_table,
    stacked,
    blocks,
    halves,
    in_sem,
    pair_sem,
    a_send,
    a_recv,
    ta_send,
    ta_recv,
    b_send,
    b_recv,
    s_send,
    s_recv,
):
    loads = [
        pltpu.make_async_copy(source, target, in_sem.at[n])
        for n, (source, target) in enumerate(
            [
                (bases_in, bases),
                (leaf_transfer_in, leaf_transfer),
                (top_transfer_in, top_transfer),
                (couplings_in, couplings),
                (top_couplings_in, top_couplings),
                (coupling_target_in, coupling_target),
                (coupling_dest_in, coupling_dest),
                (coupling_local_in, coupling_local),
                (top_target_in, top_target),
                (top_source_in, top_source),
            ]
        )
    ]
    for copy in loads:
        copy.start()

    me = lax.axis_index("leaf")
    near = lax.axis_index("near")
    core = me % 2
    y = (me // 2) % RING
    z = me // (2 * RING)
    a = z + core * (y - z)
    b = y + core * (z - y)

    def device(a_at, b_at):
        first = a_at + core * (b_at - a_at)
        second = b_at + core * (a_at - b_at)
        return {"leaf": (first * RING + second) * 2 + core}

    def wrap(value):
        return (value + 2 * RING) % RING

    b_right, b_left = device(a, wrap(b + 1)), device(a, wrap(b - 1))
    sibling = {"leaf": me + 1 - 2 * core}
    cousin = {"leaf": me + 2 - 4 * ((me // 2) % 2)}
    parity = core
    upper = (me // 2) % 2

    barrier = pltpu.get_barrier_semaphore()
    partners = [sibling, b_right, b_left] + [device(wrap(a + k), b) for k in range(1, RING)]
    for partner in partners:
        pl.semaphore_signal(barrier, inc=1, device_id=partner, device_id_type=MESH)

    def remote(source, target, send, recv, to):
        return pltpu.make_async_remote_copy(
            src_ref=source,
            dst_ref=target,
            send_sem=send,
            recv_sem=recv,
            device_id=to,
            device_id_type=MESH,
        )

    def row_of(b_at, a_at):
        return core * 64 + b_at * RING + a_at

    started = []

    def go(copy):
        copy.start()
        started.append(copy)

    row = lax.broadcasted_iota(jnp.int32, (64, 128), 0)
    lane = lax.broadcasted_iota(jnp.int32, (64, 128), 1)
    keep = row <= lane % 64
    low_lane = lane < 64
    unit = jnp.where(row == lane - 64, 1.0, 0.0)
    row32 = lax.broadcasted_iota(jnp.int32, (32, 128), 0)
    lane32 = lax.broadcasted_iota(jnp.int32, (32, 128), 1)

    for n in range(20):
        work[n] = unit
    loads[0].wait()
    loads[1].wait()
    for n in range(8):
        gram = tn(bases[n], bases[n])
        work[n, :, 0:64] = gram
        h_mine[n] = tn(leaf_transfer[n], nn(gram, leaf_transfer[n]))
    pl.semaphore_wait(barrier, len(partners))
    to_sibling = remote(h_mine, h_theirs, pair_sem.at[0], pair_sem.at[1], sibling)
    to_sibling.start()

    for panel in range(4):
        eliminate_panel(work, 0, 8, panel)

    to_sibling.wait()
    loads[2].wait()
    for n in range(8):
        work[8 + n, :, 0:64] = h_mine[n] + h_theirs[n]
    for n in range(4):
        mid = work[8 + parity * 4 + n][:, 0:64]
        k_mine[n] = tn(top_transfer[n], nn(mid, top_transfer[n]))
    to_cousin = remote(k_mine, k_theirs, pair_sem.at[2], pair_sem.at[3], cousin)
    to_cousin.start()

    for panel in range(4, 8):
        eliminate_panel(work, 0, 8, panel)

    def pair_of(first, second):
        both = jnp.where(low_lane, first, pltpu.roll(second, 64, 1))
        return jnp.where(keep, both, 0.0).astype(BF16)

    for g in range(2):
        f0, f1, f2, f3 = (work[4 * g + i] for i in range(4))
        tile = row_of(b, a) * 6 + 3 * g
        table[tile] = pair_of(f0, f1)[0:32]
        table[tile + 1] = pair_of(f2, f3)[0:32]
        corner = jnp.where(
            lane32 < 64,
            jnp.where(lane32 < 32, pltpu.roll(f0[32:64], 96, 1), f1[32:64]),
            jnp.where(lane32 < 96, pltpu.roll(f2[32:64], 32, 1), pltpu.roll(f3[32:64], 64, 1)),
        )
        table[tile + 2] = jnp.where(row32 <= lane32 % 32, corner, 0.0).astype(BF16)

    def own_sends(span, send, recv):
        for k in (1, 7, 2, 6, 3, 5, 4):
            go(remote(span, span, send.at[k], recv.at[k], device(wrap(a + k), b)))

    offsets = [0, 1, -1, 2, -2, 3, -3, 4]

    def own_arrival(w, span_of, send, recv):
        if w > 0:
            k = offsets[w] % RING
            span = span_of(wrap(a - k))
            remote(span, span, send.at[k], recv.at[k], sibling).wait_recv()

    def leaf_item(a_at):
        return table.at[pl.ds(row_of(b, a_at) * 6, 6)]

    def top_item(a_at):
        return top_table.at[row_of(b, a_at)]

    def span_at(b_at, piece, part=None):
        if piece < 8:
            return table.at[pl.ds(row_of(b_at, wrap(a - offsets[piece])) * 6, 6)]
        low, size = (0, 8) if part is None else (4 * part, 4)
        return top_table.at[pl.ds(row_of(b_at, 0) + low, size)]

    def hop(h, piece, way):
        if h == 4 and piece < 8 and (piece % 2 == 0) != (way > 0):
            return None
        return h, piece, (way < 0) * 1 if h == 4 else None

    def b_slot(h, piece, way):
        return ((h - 1) * 2 + (way > 0)) * 9 + piece

    def forward(h, piece):
        for way in (1, -1):
            kind = hop(h + 1, piece, way)
            if kind is not None:
                span = span_at(wrap(b - way * h), piece, kind[2])
                slot = b_slot(h + 1, piece, way)
                to = b_right if way > 0 else b_left
                go(remote(span, span, b_send.at[slot], b_recv.at[slot], to))

    def arrive(h, piece):
        for way in (1, -1):
            kind = hop(h, piece, way)
            if kind is not None:
                span = span_at(wrap(b - way * h), piece, kind[2])
                slot = b_slot(h, piece, way)
                remote(span, span, b_send.at[slot], b_recv.at[slot], sibling).wait_recv()

    b_offsets = [0, -1, 1, -2, 2, -3, 3, 4]

    def row_span(place, part):
        if part < 2:
            return table.at[pl.ds((place + 4 * part) * 6, 24)]
        return top_table.at[pl.ds(place, 8)]

    def hand_over(h, part):
        for slot, offset in enumerate(b_offsets):
            if abs(offset) == h:
                span = row_span(row_of(wrap(b + offset), 0), part)
                at = slot * 3 + part
                go(remote(span, span, s_send.at[at], s_recv.at[at], sibling))

    def handed(part):
        for slot, offset in enumerate(b_offsets):
            span = row_span((1 - core) * 64 + wrap(a + offset) * RING, part)
            at = slot * 3 + part
            remote(span, span, s_send.at[at], s_recv.at[at], sibling).wait_recv()

    def second_ring(h, piece):
        if h > 0:
            arrive(h, piece)
        elif piece < 8:
            own_arrival(piece, leaf_item, a_send, a_recv)
        else:
            for w in range(8):
                own_arrival(w, top_item, ta_send, ta_recv)
        if h < 4:
            forward(h, piece)
        if piece == 7:
            hand_over(h, 0)
            hand_over(h, 1)
        elif piece == 8:
            hand_over(h, 2)

    def factor(n):
        return jnp.where(keep, work[n], 0.0)[:, 0:64]

    def inverse_transposed(n):
        return work[n][:, 64:128]

    def finish_bases():
        for k in range(2):
            at = near * 2 + k
            leaf_bases[k] = nt(bases[at], inverse_transposed(at))

    def finish_leaf(n):
        piece = nn(factor(n), leaf_transfer[n])
        leaf_transfers[n] = nt(piece, inverse_transposed(8 + n))

    def finish_top(n):
        piece = nn(factor(8 + parity * 4 + n), top_transfer[n])
        top_transfers[n] = nt(piece, inverse_transposed(16 + n))

    def stack_factors():
        for n in range(8):
            low = factor(n).astype(BF16)
            stacked[n] = jnp.concatenate([low[:, :32], low[:, 32:]], 0)

    def unpack_blocks(first, last):
        for k in range(first, last):
            slab = jnp.concatenate([couplings[k].astype(F32), couplings[k + 32].astype(F32)], 0)
            blocks[pl.ds(k, 128, stride=32), :] = jnp.transpose(slab)

    def half_step(first, last):
        for n in range(first, last):
            block = blocks[32 * n : 32 * n + 32, :].astype(BF16)
            both = nn(stacked[coupling_target[n]], block, None)
            mixed = jnp.where(low_lane, both[0:64], both[64:128])
            mixed = mixed + pltpu.roll(mixed, 64, 1)
            right = jnp.where((lane // 32) % 2 == 1, mixed, pltpu.roll(mixed, 32, 1))
            local = coupling_local[n] & 3
            mixed = jnp.where(lane // 64 == (local & 1), mixed, 0.0)
            right = jnp.where(lane // 32 == local, right, 0.0)
            halves[n, :, 0:128] = mixed.astype(BF16)
            halves[n, :, 128:256] = right.astype(BF16)

    own_sends(leaf_item(a), a_send, a_recv)
    second_ring(0, 0)

    to_cousin.wait()
    for n in range(4):
        work[16 + n, :, 0:64] = k_mine[n] + k_theirs[n]
    for panel in range(8):
        eliminate_panel(work, 16, 4, panel)

    top_table[row_of(b, a)] = pair_of(work[16 + upper * 2], work[17 + upper * 2])
    own_sends(top_item(a), ta_send, ta_recv)

    for copy in loads[3:]:
        copy.wait()
    stack_factors()

    queue = [functools.partial(unpack_blocks, k, k + 4) for k in range(0, 32, 4)]
    queue += [functools.partial(half_step, n, n + 8) for n in range(0, 128, 8)]
    queue += [functools.partial(eliminate_panel, work, 8, 8, panel) for panel in range(8)]
    queue += [finish_bases]
    queue += [functools.partial(finish_leaf, n) for n in range(8)]
    queue += [functools.partial(finish_top, n) for n in range(4)]

    leaf_events = [(h, w) for h in range(5) for w in range(8)][1:]
    events = []
    for h, w in sorted(leaf_events, key=lambda at: (at[1] + 6 * at[0], -at[0])):
        events.append((h, w))
        if h == 0 and w == 7:
            events.append((0, 8))
        if h > 1 and w == 3:
            events.append((h - 1, 8))
    events.append((4, 8))
    for h, piece in events:
        second_ring(h, piece)
        if queue:
            queue.pop(0)()
    while queue:
        queue.pop(0)()

    handed(0)
    handed(1)

    def table_row(leaf_place):
        c = leaf_place & 1
        y_at = (leaf_place >> 1) & 7
        z_at = leaf_place >> 4
        return c * 64 + (y_at + c * (z_at - y_at)) * RING + z_at + c * (y_at - z_at)

    empty = jnp.zeros((32, 128), BF16)
    for n in range(128):
        local = coupling_local[n]
        tile = table_row(coupling_dest[n]) * 6 + (local >> 2) * 3
        upper_rows = jnp.concatenate([table[tile + ((local >> 1) & 1)], empty], 1)
        lower_rows = jnp.concatenate([empty, table[tile + 2]], 1)
        new = nt(halves[n], jnp.concatenate([upper_rows, lower_rows], 0), None)
        blocks[32 * n : 32 * n + 32, :] = jnp.concatenate([new[0:32], new[32:64]], 1)
    for k in range(32):
        slab = jnp.transpose(blocks[pl.ds(k, 128, stride=32), :]).astype(BF16)
        new_couplings[k] = slab[0:64]
        new_couplings[k + 32] = slab[64:128]

    handed(2)
    quad = me // 4

    def top_tile(cluster):
        place = (cluster >> 3) * 4 + (cluster & 2) + ((cluster >> 2) & 1)
        return top_table[table_row(place)]

    for n in range(16):
        target = quad * 8 + top_target[n]
        source = top_source[n]
        left = jnp.where((lane // 64) == (target & 1), top_tile(target), jnp.zeros((), BF16))
        block = top_couplings[n]
        double = jnp.concatenate([block, block], 1)
        half = nn(left, jnp.concatenate([double, double], 0), None)
        half = jnp.where((lane // 64) == (source & 1), half, 0.0).astype(BF16)
        new_top[n] = nt(half, top_tile(source), None).astype(BF16)

    for copy in started:
        copy.wait_send()


def hand_out(*refs):
    sources, targets, held = refs[0:5], refs[5:10], refs[10:15]
    in_sem, out_sem = refs[15:]
    pieces = [(3, pl.ds(16 * n, 16)) for n in range(4)]
    pieces += [(n, pl.ds(0, sources[n].shape[0])) for n in (1, 4, 2, 0)]
    arrivals, departures = [], []
    for at, (n, span) in enumerate(pieces):
        inward = pltpu.make_async_copy(sources[n].at[span], held[n].at[span], in_sem.at[at])
        inward.start()
        arrivals.append(inward)
        departures.append(
            pltpu.make_async_copy(held[n].at[span], targets[n].at[span], out_sem.at[at])
        )
    for inward, outward in zip(arrivals, departures):
        inward.wait()
        outward.start()
    for outward in departures:
        outward.wait()


def on_device(
    bases,
    leaf_transfer,
    top_transfer,
    couplings,
    coupling_target,
    coupling_dest,
    coupling_local,
    top_couplings,
    top_target,
    top_source,
):
    vmem = pl.BlockSpec(memory_space=pltpu.VMEM)
    anywhere = pl.BlockSpec(memory_space=pl.ANY)
    dma = pltpu.SemaphoreType.DMA
    shapes = (
        jax.ShapeDtypeStruct((2, 64, 64), F32),
        jax.ShapeDtypeStruct((8, 64, 64), F32),
        jax.ShapeDtypeStruct((4, 64, 64), F32),
        jax.ShapeDtypeStruct((64, 64, 128), BF16),
        jax.ShapeDtypeStruct((16, 64, 64), BF16),
    )
    results = pl.pallas_call(
        kernel,
        out_shape=shapes,
        in_specs=[anywhere] * 10,
        out_specs=[vmem] * 5,
        scratch_shapes=[
            pltpu.VMEM((8, 64, 64), F32),
            pltpu.VMEM((8, 64, 64), F32),
            pltpu.VMEM((4, 64, 64), F32),
            pltpu.VMEM((64, 64, 128), BF16),
            pltpu.VMEM((16, 64, 64), BF16),
            pltpu.SMEM((128,), jnp.int32),
            pltpu.SMEM((128,), jnp.int32),
            pltpu.SMEM((128,), jnp.int32),
            pltpu.SMEM((16,), jnp.int32),
            pltpu.SMEM((16,), jnp.int32),
            pltpu.VMEM((20, 64, 128), F32),
            pltpu.VMEM((8, 64, 64), F32),
            pltpu.VMEM((8, 64, 64), F32),
            pltpu.VMEM((4, 64, 64), F32),
            pltpu.VMEM((4, 64, 64), F32),
            pltpu.VMEM((768, 32, 128), BF16),
            pltpu.VMEM((128, 64, 128), BF16),
            pltpu.VMEM((8, 128, 32), BF16),
            pltpu.VMEM((4096, 128), F32),
            pltpu.VMEM((128, 64, 256), BF16),
            dma((10,)),
            dma((4,)),
            dma((8,)),
            dma((8,)),
            dma((8,)),
            dma((8,)),
            dma((72,)),
            dma((72,)),
            dma((24,)),
            dma((24,)),
        ],
        compiler_params=pltpu.CompilerParams(
            collective_id=0, has_side_effects=True, vmem_limit_bytes=58 * 2**20
        ),
    )(
        bases,
        leaf_transfer,
        top_transfer,
        jnp.transpose(couplings, (1, 2, 0)),
        top_couplings,
        coupling_target,
        coupling_dest[:, 0],
        coupling_local,
        top_target,
        top_source,
    )
    leaf_bases, leaf_transfers, top_transfers, new_couplings, new_top = pl.pallas_call(
        hand_out,
        out_shape=shapes,
        in_specs=[anywhere] * 5,
        out_specs=[anywhere] * 5,
        scratch_shapes=[pltpu.VMEM(shape.shape, shape.dtype) for shape in shapes]
        + [dma((8,)), dma((8,))],
        compiler_params=pltpu.CompilerParams(vmem_limit_bytes=58 * 2**20),
    )(*results)
    return (
        leaf_bases,
        leaf_transfers,
        top_transfers,
        jnp.transpose(new_couplings, (2, 0, 1)),
        new_top,
    )


def solution(mesh):
    in_specs = (
        P("leaf", None, None),
        P("leaf", None, None),
        P("leaf", None, None),
        P(("leaf", "near"), None, None),
        P(("leaf", "near")),
        P(("leaf", "near"), None),
        P(("leaf", "near")),
        P(("leaf", "near"), None, None),
        P(("leaf", "near")),
        P(("leaf", "near")),
    )
    out_specs = (
        P(("leaf", "near"), None, None),
        P("leaf", None, None),
        P("leaf", None, None),
        P(("leaf", "near"), None, None),
        P(("leaf", "near"), None, None),
    )
    return jax.shard_map(
        on_device, mesh=mesh, in_specs=in_specs, out_specs=out_specs, check_vma=False
    )
```
